512 devices in a mesh: row: 32 (over z_hi, x, core), col: 16 (over y, z_lo).
Axes of the slice: x: 4, y: 4, z: 16 (z_hi: 4, z_lo: 4; z = z_hi * 4 + z_lo), core: 2. Of those that a mesh axis runs over, the one named last changes fastest.
Arguments:
- right_sides: float32 [8, 131072], P(None, ('row', 'col')), may hold values from -11 to 11
- noise_var: float32 [131072], P(('row', 'col')), may hold values from 1.2 to 3
- observed: int32 [131072], P(('row', 'col')), may hold values 0 or 1
- tile_data: bfloat16 [32, 16, 32, 128, 128], P('row', 'col'), may hold values from -1 to 1
- diag_tiles: bfloat16 [1024, 128, 128], P(('row', 'col')), may hold values from -1 to 1
- tile_rows: int32 [32, 16, 32], P('row', 'col'), may hold values from 0 to 63
- tile_cols: int32 [32, 16, 32], P('row', 'col'), may hold values from 0 to 31
- tile_count: int32 [32, 16], P('row', 'col'), may hold values from 16 to 32, as said below
Outputs:
- solution: float32 [8, 131072], P(None, ('row', 'col'))
- residual: float32 [8, 131072], P(None, ('row', 'col'))
The draws below stay inside these ranges and needn't reach their ends.
Inputs may be any that keep to these rules, and one draw needn't show every extreme that they name: A device's slots t < tile_count name distinct pairs (i, j) whose blocks satisfy I != J, with I < J exactly when I + J is even, so that each pair of blocks is stored at most once; slots beyond the count hold arbitrary indices in range. Every device of the last row has exactly 32 live slots.
All inputs are finite; a program needn't handle non-finite values. No bound on the sum of `observed` on one device may be relied on, other than what follows from the above.
Results may differ from the reference program's by a relative error of at most 0.0003.
Values sent between devices are 32-bit elements; how exact they have to be, the bound alone decides.
A program may use at most 64 MiB of HBM per device.

```python
import math
import jax
import jax.numpy as jnp
from jax import lax

TILE = 128
COUPLED = 32
NRHS = 8
ITERS = 2
BLK_DEV = 2
TILES_DEV = 32
NBLK = 1024
NPIX = 131072
N_ROW = 32
N_COL = 16


def layout(key):
    base_key = jax.random.fold_in(key, 11)
    rows_here = N_ROW * BLK_DEV
    cols_here = N_COL * BLK_DEV
    pair_total = rows_here * cols_here
    device_row = jnp.arange(N_ROW, dtype=jnp.int32)[:, None, None, None]
    device_col = jnp.arange(N_COL, dtype=jnp.int32)[None, :, None, None]
    local_i = jnp.arange(rows_here, dtype=jnp.int32)[None, None, :, None]
    local_j = jnp.arange(cols_here, dtype=jnp.int32)[None, None, None, :]
    block_i = (local_i // BLK_DEV * N_COL + device_col) * BLK_DEV + local_i % BLK_DEV
    block_j = (device_row * N_COL + local_j // BLK_DEV) * BLK_DEV + local_j % BLK_DEV
    even_pair = (block_i + block_j) % 2 == 0
    is_valid = (block_i != block_j) & ((block_i < block_j) == even_pair)
    shape = (N_ROW, N_COL, rows_here, cols_here)
    flat_index = jnp.broadcast_to(local_i * cols_here + local_j, shape).astype(jnp.int32)
    spread = max(2 ** 30 // pair_total, 2)
    scores = jax.random.randint(jax.random.fold_in(base_key, 1), shape, 0, spread, dtype=jnp.int32) * pair_total + flat_index
    scores = jnp.where(is_valid, scores, 2 ** 30 + flat_index).astype(jnp.int32)
    ranking = jnp.argsort(scores.reshape(N_ROW, N_COL, pair_total), axis=-1, stable=True)[:, :, :TILES_DEV]
    ranking = ranking.astype(jnp.int32)
    row_pick = (ranking // cols_here).astype(jnp.int32)
    col_pick = (ranking % cols_here).astype(jnp.int32)
    valid_count = jnp.sum(is_valid.astype(jnp.int32), axis=(2, 3)).astype(jnp.int32)
    drawn_count = jax.random.randint(jax.random.fold_in(base_key, 2), (N_ROW, N_COL), TILES_DEV // 2, TILES_DEV + 1, dtype=jnp.int32)
    last_row = jnp.arange(N_ROW, dtype=jnp.int32)[:, None] == N_ROW - 1
    first_device = (jnp.arange(N_ROW, dtype=jnp.int32)[:, None] == 0) & (jnp.arange(N_COL, dtype=jnp.int32)[None, :] == 0)
    chosen = jnp.where(first_device, TILES_DEV // 2, drawn_count)
    chosen = jnp.where(last_row, TILES_DEV, chosen)
    live_count = jnp.minimum(chosen, valid_count).astype(jnp.int32)
    return (row_pick, col_pick, live_count)


def draw_tile_rows(key, part):
    return layout(key)[0]


def draw_tile_cols(key, part):
    return layout(key)[1]


def draw_tile_count(key, part):
    return layout(key)[2]


def draw_tile_data(key, part):
    values = jax.random.uniform(jax.random.fold_in(key, 31), (N_ROW, N_COL, TILES_DEV, TILE, TILE), jnp.float32, -1.0, 1.0)
    return values.astype(jnp.bfloat16)


def draw_diag_tiles(key, part):
    values = jax.random.uniform(jax.random.fold_in(key, 41), (NBLK, TILE, TILE), jnp.float32, -1.0, 1.0)
    return values.astype(jnp.bfloat16)


def draw_right_sides(key, part):
    first_key = jax.random.fold_in(key, 21)
    second_key = jax.random.fold_in(key, 22)
    position = jnp.arange(NPIX, dtype=jnp.float32)[None, :] / NPIX
    offset = jax.random.uniform(first_key, (NRHS, 1), jnp.float32, -0.5, 0.5)
    rough = jnp.clip(jax.random.normal(second_key, (NRHS, NPIX), jnp.float32), -3.0, 3.0)
    scale = 1.0 + 2.0 * position
    return (scale * (offset + rough)).astype(jnp.float32)


def with_ends(result, own_key, low, high):
    spot = [jax.random.randint(jax.random.fold_in(own_key, axis), (), 0, length) for axis, length in enumerate(result.shape)]
    main_axis = result.shape.index(max(result.shape))
    beside = spot[:main_axis] + [(spot[main_axis] + 1) % result.shape[main_axis]] + spot[main_axis + 1:]
    return result.at[tuple(spot)].set(low).at[tuple(beside)].set(high)


def steps_of(rng, extent, split, low, top_value):
    def one(axis_at, blocks):
        heights = jax.random.uniform(jax.random.fold_in(jax.random.fold_in(rng, 6), axis_at), (blocks,), jnp.float32, low / len(split), top_value / len(split))
        return jnp.repeat(jnp.exp(heights), extent[axis_at] // blocks).reshape((-1,) + (1,) * (len(extent) - axis_at - 1))

    level = one(*split[0])
    for cut in split[1:]:
        level = level * one(*cut)
    return level


def setup_inputs(seed: int = 0) -> dict:
    key_list = jax.random.split(jax.random.key(seed), 9)
    return {
        "right_sides": draw_right_sides(jax.random.fold_in(key_list[8], 71), 0),
        "noise_var": jnp.clip(jnp.exp(math.log(3.0) - 0.9162907 * jax.random.uniform(key_list[1], (NPIX,), jnp.float32) ** steps_of(key_list[1], (NPIX,), ((0, 512),), -0.2, 0.2)), 1.2, 3.0),
        "observed": with_ends((jax.random.randint(key_list[2], (NPIX,), 0, 4) < 3).astype(jnp.int32), jax.random.fold_in(key_list[2], 1), 0, 1),
        "tile_data": draw_tile_data(jax.random.fold_in(key_list[8], 71), 0),
        "diag_tiles": draw_diag_tiles(jax.random.fold_in(key_list[8], 71), 0),
        "tile_rows": draw_tile_rows(jax.random.fold_in(key_list[8], 71), 0),
        "tile_cols": draw_tile_cols(jax.random.fold_in(key_list[8], 71), 0),
        "tile_count": draw_tile_count(jax.random.fold_in(key_list[8], 71), 0),
    }


def upper_masks(size):
    row_index = jnp.arange(size)[:, None]
    col_index = jnp.arange(size)[None, :]
    return ((col_index >= row_index).astype(jnp.float32), (col_index > row_index).astype(jnp.float32))

def operate(field_in, observed_float, noise_var, tile_data, diag_tiles, tile_rows, tile_cols, tile_count):
    coupling = 1.0 / (2.0 * math.sqrt(TILE * (2 * COUPLED + 1)))
    block_total = NPIX // TILE
    masked = (observed_float[None, :] * field_in).reshape(NRHS, block_total, TILE)
    with_diag, strict = upper_masks(TILE)
    diag_float = diag_tiles.astype(jnp.float32)
    coupled = jnp.einsum('kab,skb->ska', diag_float * with_diag, masked, precision=lax.Precision.HIGHEST)
    coupled = coupled + jnp.einsum('kab,ska->skb', diag_float * strict, masked, precision=lax.Precision.HIGHEST)
    devices = N_ROW * N_COL
    flat_tiles = tile_data.reshape(devices, TILES_DEV, TILE, TILE)
    flat_rows = tile_rows.reshape(devices, TILES_DEV)
    flat_cols = tile_cols.reshape(devices, TILES_DEV)
    flat_count = tile_count.reshape(devices)

    def visit_device(running, inputs):
        device_index, dev_tiles, dev_rows, dev_cols, dev_count = inputs
        device_row = device_index // N_COL
        device_col = device_index % N_COL
        live_slots = (jnp.arange(TILES_DEV) < dev_count).astype(jnp.float32)[None, :, None]
        block_i = ((dev_rows // BLK_DEV * N_COL + device_col) * BLK_DEV + dev_rows % BLK_DEV).astype(jnp.int32)
        block_j = ((device_row * N_COL + dev_cols // BLK_DEV) * BLK_DEV + dev_cols % BLK_DEV).astype(jnp.int32)
        tile_float = dev_tiles.astype(jnp.float32)
        upper_terms = jnp.einsum('tab,stb->sta', tile_float, masked[:, block_j, :], precision=lax.Precision.HIGHEST) * live_slots
        lower_terms = jnp.einsum('tab,sta->stb', tile_float, masked[:, block_i, :], precision=lax.Precision.HIGHEST) * live_slots
        running = running.at[:, block_i, :].add(upper_terms)
        running = running.at[:, block_j, :].add(lower_terms)
        return (running, None)
    start = jnp.zeros((NRHS, block_total, TILE), jnp.float32)
    device_ids = jnp.arange(devices, dtype=jnp.int32)
    offdiag, _ = lax.scan(visit_device, start, (device_ids, flat_tiles, flat_rows, flat_cols, flat_count))
    total = (coupled + offdiag).reshape(NRHS, NPIX)
    return noise_var[None, :] * field_in + observed_float[None, :] * (coupling * total)

def reference(right_sides, noise_var, observed, tile_data, diag_tiles, tile_rows, tile_cols, tile_count):
    observed_float = observed.astype(jnp.float32)

    def apply_operator(field_in):
        return operate(field_in, observed_float, noise_var, tile_data, diag_tiles, tile_rows, tile_cols, tile_count)
    solution = jnp.zeros_like(right_sides)
    residual = right_sides
    direction = right_sides
    norm_now = lax.optimization_barrier(jnp.sum(residual * residual, axis=1))
    for iteration in range(ITERS):
        image_field = apply_operator(direction)
        step_alpha = norm_now / lax.optimization_barrier(jnp.sum(direction * image_field, axis=1))
        solution = solution + step_alpha[:, None] * direction
        residual = residual - step_alpha[:, None] * image_field
        norm_next = lax.optimization_barrier(jnp.sum(residual * residual, axis=1))
        direction = residual + (norm_next / norm_now)[:, None] * direction
        norm_now = norm_next
    return (solution, residual)
```

```python
import functools
import math

import jax
import jax.numpy as jnp
from jax import lax
from jax.experimental import pallas as pl
from jax.experimental.pallas import tpu as pltpu
from jax.sharding import PartitionSpec as P

TILE = 128
COUPLED = 32
NRHS = 8
MESH = pl.DeviceIdType.MESH
ROW_PARTS = (4, 4, 2)
COL_PARTS = (4, 4)
F32 = jnp.float32
BF16 = jnp.bfloat16


def split_rows(value):
    high = value.astype(BF16).astype(F32)
    return jnp.concatenate([high, value - high], axis=0).astype(BF16)


def near_first(size):
    return sorted(range(1, size), key=lambda d: min(d, size - d))


def kernel(
    rparts,
    cparts,
    rs_ref,
    noise_ref,
    obs_ref,
    diag_hbm,
    tile_hbm,
    rows_s,
    cols_s,
    count_s,
    sol_ref,
    res_ref,
    tiles,
    diag,
    sym,
    hrow,
    hcol,
    rowbuf,
    colbuf,
    rowsplit,
    colsplit,
    gath,
    rowterm,
    colterm,
    xrecv,
    zsend,
    zrecv,
    yrecv,
    lsend,
    lrecv,
    red_src,
    red_dst,
    local_sem,
    agz_sem,
    agx_sem,
    agl_sem,
    agy_sem,
    rsx_sem,
    rsz_sem,
    rcy_sem,
    rcl_sem,
    red_sem,
):
    nzh, nx, nc = rparts
    ny, nzl = cparts
    nrow, ncol = nzh * nx * nc, ny * nzl
    slots = tile_hbm.shape[0]
    coupling = 1.0 / (2.0 * math.sqrt(TILE * (2 * COUPLED + 1)))

    row = lax.axis_index("row")
    col = lax.axis_index("col")
    zh, x, core = row // (nx * nc), row // nc % nx, row % nc
    y, zl = col // nzl, col % nzl

    def row_at(dz, dx, dc):
        return (
            lax.rem(zh + dz, nzh) * (nx * nc)
            + lax.rem(x + dx, nx) * nc
            + lax.rem(core + dc, nc)
        )

    def col_at(dy, dl):
        return lax.rem(y + dy, ny) * nzl + lax.rem(zl + dl, nzl)

    def row_from(dz, dx, dc):
        return row_at(nzh - dz, nx - dx, nc - dc)

    def col_from(dy, dl):
        return col_at(ny - dy, nzl - dl)

    plane = [(dx, dc) for dx in range(nx) for dc in range(nc) if dx or dc]
    plane = sorted(plane, key=lambda p: -min(p[0], nx - p[0]))
    line = [(dz, dl) for dz in range(nzh) for dl in range(nzl) if dz or dl]
    line = sorted(line, key=lambda p: -min(p[0] * nzl + p[1], nzh * nzl - p[0] * nzl - p[1]))
    zs, ys, ls = near_first(nzh), near_first(ny), list(range(1, nzl))

    barrier = pltpu.get_barrier_semaphore()
    peers = [(row_at(dz, 0, 0), col_at(0, dl)) for dz, dl in line]
    peers += [(row_at(0, dx, dc), col) for dx, dc in plane]
    peers += [(row, col_at(dy, 0)) for dy in ys]
    for peer in peers:
        pl.semaphore_signal(barrier, inc=1, device_id=peer, device_id_type=MESH)

    pending = []

    def remote(src, dst, sems, index, device):
        return pltpu.make_async_remote_copy(
            src_ref=src,
            dst_ref=dst,
            send_sem=sems.at[(0, *index)],
            recv_sem=sems.at[(1, *index)],
            device_id=device,
            device_id_type=MESH,
        )

    def send(src, dst, sems, index, device):
        copy = remote(src, dst, sems, index, device)
        copy.start()
        pending.append(copy)

    def arrive(dst, sems, index):
        remote(dst, dst, sems, index, (row, col)).wait_recv()

    tile_copy = pltpu.make_async_copy(tile_hbm, tiles, local_sem.at[0])
    diag_copy = pltpu.make_async_copy(diag_hbm, diag, local_sem.at[1])
    diag_copy.start()
    tile_copy.start()

    observed = [obs_ref[:, k * TILE : (k + 1) * TILE].astype(F32) for k in range(2)]
    noise = [noise_ref[:, k * TILE : (k + 1) * TILE] for k in range(2)]
    right = [rs_ref[:, k * TILE : (k + 1) * TILE] for k in range(2)]

    def chunk_row(it, r):
        return rowbuf.at[it, pl.ds(2 * r, 2)]

    def chunk_col(it, c):
        return colbuf.at[it, pl.ds(2 * c, 2)]

    def put_masked(it, masked):
        for k in range(2):
            rowbuf[it, 2 * row + k] = masked[k]
            colbuf[it, 2 * col + k] = masked[k]

    def start_gather(it):
        mine_r, mine_c = chunk_row(it, row), chunk_col(it, col)
        for d in reversed(zs):
            send(mine_r, mine_r, agz_sem, (it, d), (row_at(d, 0, 0), col))
        for d in ls:
            send(mine_c, mine_c, agl_sem, (it, d), (row, col_at(0, d)))
        for d in ys:
            send(mine_c, mine_c, agy_sem, (it, 0, d), (row, col_at(d, 0)))
        for dx, dc in plane:
            send(mine_r, mine_r, agx_sem, (it, 0, dx * nc + dc), (row_at(0, dx, dc), col))

    def col_forward(it, d):
        got = chunk_col(it, col_from(0, d))
        arrive(got, agl_sem, (it, d))
        for dy in ys:
            send(got, got, agy_sem, (it, d, dy), (row, col_at(dy, 0)))

    def row_forward(it, d):
        got = chunk_row(it, row_from(d, 0, 0))
        arrive(got, agz_sem, (it, d))
        for dx, dc in plane:
            send(got, got, agx_sem, (it, d, dx * nc + dc), (row_at(0, dx, dc), col))

    def col_done(it):
        for d in range(nzl):
            for dy in ys:
                arrive(chunk_col(it, col_from(dy, d)), agy_sem, (it, d, dy))

    def row_done(it):
        for d in [0, *zs]:
            for dx, dc in plane:
                arrive(
                    chunk_row(it, row_from(d, dx, dc)), agx_sem, (it, d, dx * nc + dc)
                )

    def product(hot, value):
        high = value.astype(BF16)
        low = (value - high.astype(F32)).astype(BF16)
        both = jnp.concatenate([high, low], axis=1)
        sums = jnp.dot(hot, both, preferred_element_type=F32)
        return sums[:, :TILE] + sums[:, TILE:]

    def terms(picks, pieces, contract):
        for t in range(slots):
            gath[t] = pieces[picks[t]]
        out = lax.dot_general(
            gath[...],
            tiles[...],
            (((2,), (contract,)), ((0,), (0,))),
            preferred_element_type=F32,
        )
        return (out[:, :NRHS] + out[:, NRHS:]).reshape(slots * NRHS, TILE)

    def upper(it):
        for j in range(2 * ncol):
            colsplit[j] = split_rows(colbuf[it, j])
        value = terms(cols_s, colsplit, 2)
        rowterm[it] = product(hrow[...], value).reshape(2 * nrow, NRHS, TILE)
        for dz in [*reversed(zs), 0]:
            for dx, dc in plane:
                send(
                    rowterm.at[it, pl.ds(2 * row_at(dz, dx, dc), 2)],
                    xrecv.at[it, dz, dx * nc + dc],
                    rsx_sem,
                    (it, dz, dx * nc + dc),
                    (row_at(0, dx, dc), col),
                )

    def lower(it):
        for i in range(2 * nrow):
            rowsplit[i] = split_rows(rowbuf[it, i])
        value = terms(rows_s, rowsplit, 1)
        colterm[it] = product(hcol[...], value).reshape(2 * ncol, NRHS, TILE)
        for dl in [*ls, 0]:
            for dy in ys:
                send(
                    colterm.at[it, pl.ds(2 * col_at(dy, dl), 2)],
                    yrecv.at[it, dl, dy],
                    rcy_sem,
                    (it, dl, dy),
                    (row, col_at(dy, 0)),
                )

    def row_reduce(it, dz):
        for dx, dc in plane:
            arrive(xrecv.at[it, dz, dx * nc + dc], rsx_sem, (it, dz, dx * nc + dc))
        total = rowterm[it, pl.ds(2 * row_at(dz, 0, 0), 2)]
        for dx, dc in plane:
            total = total + xrecv[it, dz, dx * nc + dc]
        zsend[it, dz] = total
        if dz:
            send(zsend.at[it, dz], zrecv.at[it, dz], rsz_sem, (it, dz), (row_at(dz, 0, 0), col))

    def col_reduce(it, dl):
        for dy in ys:
            arrive(yrecv.at[it, dl, dy], rcy_sem, (it, dl, dy))
        total = colterm[it, pl.ds(2 * col_at(0, dl), 2)]
        for dy in ys:
            total = total + yrecv[it, dl, dy]
        lsend[it, dl] = total
        if dl:
            send(lsend.at[it, dl], lrecv.at[it, dl], rcl_sem, (it, dl), (row, col_at(0, dl)))

    def row_final(it):
        total = zsend[it, 0]
        for d in zs:
            arrive(zrecv.at[it, d], rsz_sem, (it, d))
            total = total + zrecv[it, d]
        return total

    def col_final(it):
        total = lsend[it, 0]
        for d in ls:
            arrive(lrecv.at[it, d], rcl_sem, (it, d))
            total = total + lrecv[it, d]
        return total

    lane = lax.broadcasted_iota(jnp.int32, (NRHS, TILE), 1)
    sub = lax.broadcasted_iota(jnp.int32, (NRHS, TILE), 0)
    stages = (
        [(dx * nc + dc, (row_at(0, dx, dc), col)) for dx, dc in plane],
        [(dy, (row, col_at(dy, 0))) for dy in ys],
        [(dz * nzl + dl, (row_at(dz, 0, 0), col_at(0, dl))) for dz, dl in line],
    )

    def red_send(r, stage, value):
        red_src[r, stage] = value
        for slot, device in stages[stage]:
            send(
                red_src.at[r, stage],
                red_dst.at[r, stage, slot],
                red_sem,
                (r, stage, slot),
                device,
            )

    def red_get(r, stage):
        for slot, _ in stages[stage]:
            arrive(red_dst.at[r, stage, slot], red_sem, (r, stage, slot))
        total = red_src[r, stage]
        for slot, _ in stages[stage]:
            total = total + red_dst[r, stage, slot]
        return total

    def pack(values):
        packed = jnp.zeros((NRHS, TILE), F32)
        for k, value in enumerate(values):
            whole = jnp.sum(value, axis=1, keepdims=True)
            packed = packed + jnp.where(lane == sub + NRHS * k, whole, 0.0)
        return jnp.sum(packed, axis=0, keepdims=True)

    def unpack(total, k):
        return jnp.sum(jnp.where(lane == sub + NRHS * k, total, 0.0), axis=1, keepdims=True)

    put_masked(0, [observed[k] * right[k] for k in range(2)])
    wide = lax.broadcasted_iota(jnp.int32, (1, slots * NRHS), 1)
    row_index = jnp.zeros((1, slots * NRHS), jnp.int32)
    col_index = jnp.zeros((1, slots * NRHS), jnp.int32)
    for t in range(slots):
        here = wide // NRHS == t
        row_index = jnp.where(here, rows_s[t] * NRHS, row_index)
        col_index = jnp.where(here, cols_s[t] * NRHS, col_index)
    live = wide // NRHS < count_s[0]
    row_index = jnp.where(live, row_index + wide % NRHS, -1)
    col_index = jnp.where(live, col_index + wide % NRHS, -1)
    step = 64

    def fill(ref, index):
        for start in range(0, ref.shape[0], step):
            at = lax.broadcasted_iota(jnp.int32, (step, slots * NRHS), 0) + start
            ref[start : start + step] = jnp.where(at == index, 1.0, 0.0).astype(BF16)

    fill(hrow, row_index)
    fill(hcol, col_index)
    diag_copy.wait()
    a_index = lax.broadcasted_iota(jnp.int32, (TILE, TILE), 0)
    b_index = lax.broadcasted_iota(jnp.int32, (TILE, TILE), 1)
    for k in range(2):
        block = diag[k].astype(F32)
        sym[k] = jnp.where(b_index >= a_index, block, block.T).astype(BF16)
    tile_copy.wait()

    def own_terms(masked):
        out = []
        for k in range(2):
            both = jnp.dot(split_rows(masked[k]), sym[k], preferred_element_type=F32)
            out.append(both[:NRHS] + both[NRHS:])
        return out

    masked_b = [observed[k] * right[k] for k in range(2)]
    diag_b = own_terms(masked_b)

    pl.semaphore_wait(barrier, len(peers))

    def gather_upper(it):
        for d in ls:
            col_forward(it, d)
        for d in zs[:-1]:
            row_forward(it, d)

    start_gather(0)
    gather_upper(0)
    col_done(0)
    upper(0)
    for d in zs[-1:]:
        row_forward(0, d)
    row_done(0)
    lower(0)
    quad = jnp.zeros((NRHS, TILE), F32)
    for i in range(2 * nrow):
        quad = quad + rowterm[0, i] * rowbuf[0, i]
    quad = 2.0 * quad
    for k in range(2):
        quad = quad + masked_b[k] * diag_b[k]
    quad = coupling * quad
    for k in range(2):
        quad = quad + noise[k] * right[k] * right[k]
    red_send(0, 0, pack([right[0] * right[0] + right[1] * right[1], quad]))
    for d in reversed(zs):
        row_reduce(0, d)
    for d in [*ls, 0]:
        col_reduce(0, d)
    row_reduce(0, 0)
    red_send(0, 1, red_get(0, 0))
    mirrored = col_final(0)
    red_send(0, 2, red_get(0, 1))
    total = row_final(0) + mirrored
    w = [
        noise[k] * right[k] + observed[k] * (coupling * (total[k] + diag_b[k]))
        for k in range(2)
    ]

    masked_w = [observed[k] * w[k] for k in range(2)]
    put_masked(1, masked_w)
    start_gather(1)
    diag_w = own_terms(masked_w)
    gather_upper(1)
    first = red_get(0, 2)
    rr0, dad0 = unpack(first, 0), unpack(first, 1)
    alpha = rr0 / dad0
    res = [right[k] - alpha * w[k] for k in range(2)]
    red_send(
        1, 0, pack([res[0] * res[0] + res[1] * res[1], res[0] * w[0] + res[1] * w[1]])
    )
    col_done(1)
    upper(1)
    for d in zs[-1:]:
        row_forward(1, d)
    red_send(1, 1, red_get(1, 0))
    row_done(1)
    quad = jnp.zeros((NRHS, TILE), F32)
    for i in range(2 * nrow):
        quad = quad + (rowterm[0, i] - alpha * rowterm[1, i]) * (
            rowbuf[0, i] - alpha * rowbuf[1, i]
        )
    quad = 2.0 * quad
    for k in range(2):
        quad = quad + (masked_b[k] - alpha * masked_w[k]) * (diag_b[k] - alpha * diag_w[k])
    quad = coupling * quad
    for k in range(2):
        quad = quad + noise[k] * res[k] * res[k]
    red_send(2, 0, pack([quad]))
    lower(1)
    red_send(1, 2, red_get(1, 1))
    for d in reversed(zs):
        row_reduce(1, d)
    red_send(2, 1, red_get(2, 0))
    for d in [*ls, 0]:
        col_reduce(1, d)
    row_reduce(1, 0)
    red_send(2, 2, red_get(2, 1))
    mirrored = col_final(1)
    total = row_final(1) + mirrored
    second = red_get(1, 2)
    rr1, rw1 = unpack(second, 0), unpack(second, 1)
    beta = rr1 / rr0
    u = [
        noise[k] * w[k] + observed[k] * (coupling * (total[k] + diag_w[k]))
        for k in range(2)
    ]
    third = unpack(red_get(2, 2), 0)
    dad1 = third + 2.0 * beta * rw1 + beta * beta * dad0
    alpha1 = rr1 / dad1
    for k in range(2):
        here = slice(k * TILE, (k + 1) * TILE)
        direction = res[k] + beta * right[k]
        image = (w[k] - alpha * u[k]) + beta * w[k]
        sol_ref[:, here] = alpha * right[k] + alpha1 * direction
        res_ref[:, here] = res[k] - alpha1 * image
    for copy in pending:
        copy.wait_send()


def local(
    rparts,
    cparts,
    right_sides,
    noise_var,
    observed,
    tile_data,
    diag_tiles,
    tile_rows,
    tile_cols,
    tile_count,
):
    slots = tile_data.shape[2]
    nzh, nx, nc = rparts
    ny, nzl = cparts
    nrow, ncol = nzh * nx * nc, ny * nzl
    vmem = pl.BlockSpec(memory_space=pltpu.VMEM)
    smem = pl.BlockSpec(memory_space=pltpu.SMEM)
    hbm = pl.BlockSpec(memory_space=pl.ANY)
    dma = pltpu.SemaphoreType.DMA
    chunk = (2, NRHS, TILE)
    shape = jax.ShapeDtypeStruct(right_sides.shape, F32)
    return pl.pallas_call(
        functools.partial(kernel, rparts, cparts),
        out_shape=(shape, shape),
        in_specs=[vmem, vmem, vmem, hbm, hbm, smem, smem, smem],
        out_specs=(vmem, vmem),
        scratch_shapes=[
            pltpu.VMEM((slots, TILE, TILE), BF16),
            pltpu.VMEM((2, TILE, TILE), BF16),
            pltpu.VMEM((2, TILE, TILE), BF16),
            pltpu.VMEM((2 * nrow * NRHS, slots * NRHS), BF16),
            pltpu.VMEM((2 * ncol * NRHS, slots * NRHS), BF16),
            pltpu.VMEM((2, 2 * nrow, NRHS, TILE), F32),
            pltpu.VMEM((2, 2 * ncol, NRHS, TILE), F32),
            pltpu.VMEM((2 * nrow, 2 * NRHS, TILE), BF16),
            pltpu.VMEM((2 * ncol, 2 * NRHS, TILE), BF16),
            pltpu.VMEM((slots, 2 * NRHS, TILE), BF16),
            pltpu.VMEM((2, 2 * nrow, NRHS, TILE), F32),
            pltpu.VMEM((2, 2 * ncol, NRHS, TILE), F32),
            pltpu.VMEM((2, nzh, nx * nc, *chunk), F32),
            pltpu.VMEM((2, nzh, *chunk), F32),
            pltpu.VMEM((2, nzh, *chunk), F32),
            pltpu.VMEM((2, nzl, ny, *chunk), F32),
            pltpu.VMEM((2, nzl, *chunk), F32),
            pltpu.VMEM((2, nzl, *chunk), F32),
            pltpu.VMEM((3, 3, 1, TILE), F32),
            pltpu.VMEM((3, 3, max(16, nx * nc), 1, TILE), F32),
            dma((2,)),
            dma((2, 2, nzh)),
            dma((2, 2, nzh, nx * nc)),
            dma((2, 2, nzl)),
            dma((2, 2, nzl, ny)),
            dma((2, 2, nzh, nx * nc)),
            dma((2, 2, nzh)),
            dma((2, 2, nzl, ny)),
            dma((2, 2, nzl)),
            dma((2, 3, 3, 16)),
        ],
        compiler_params=pltpu.CompilerParams(
            collective_id=0, has_side_effects=True, vmem_limit_bytes=48 << 20
        ),
        name="solve",
    )(
        right_sides,
        noise_var.reshape(1, -1),
        observed.reshape(1, -1),
        diag_tiles,
        tile_data.reshape(slots, TILE, TILE),
        tile_rows.reshape(slots),
        tile_cols.reshape(slots),
        tile_count.reshape(1),
    )


def solution(mesh):
    return jax.shard_map(
        functools.partial(local, ROW_PARTS, COL_PARTS),
        mesh=mesh,
        in_specs=(
            P(None, ("row", "col")),
            P(("row", "col")),
            P(("row", "col")),
            P("row", "col", None, None, None),
            P(("row", "col"), None, None),
            P("row", "col", None),
            P("row", "col", None),
            P("row", "col"),
        ),
        out_specs=(P(None, ("row", "col")), P(None, ("row", "col"))),
        check_vma=False,
    )
```

```python
import functools
import math

import jax
import jax.numpy as jnp
from jax import lax
from jax.experimental import pallas as pl
from jax.experimental.pallas import tpu as pltpu
from jax.sharding import PartitionSpec as P

TILE = 128
COUPLED = 32
NRHS = 8
MESH = pl.DeviceIdType.MESH
ROW_PARTS = (4, 4, 2)
COL_PARTS = (4, 4)
F32 = jnp.float32
BF16 = jnp.bfloat16


def split_rows(value):
    high = value.astype(BF16).astype(F32)
    return jnp.concatenate([high, value - high], axis=0).astype(BF16)


def near_first(size):
    return sorted(range(1, size), key=lambda d: min(d, size - d))


def kernel(
    rparts,
    cparts,
    rs_hbm,
    noise_hbm,
    obs_hbm,
    diag_hbm,
    tile_hbm,
    rows_hbm,
    cols_hbm,
    count_hbm,
    sol_ref,
    res_ref,
    rs_ref,
    noise_ref,
    obs_ref,
    rows_s,
    cols_s,
    count_s,
    tiles,
    diag,
    sym,
    hrow,
    hcol,
    rowbuf,
    colbuf,
    rowsplit,
    colsplit,
    gath,
    rowterm,
    colterm,
    xrecv,
    zsend,
    frecv,
    zrecv,
    yrecv,
    lsend,
    lrecv,
    red_src,
    red_dst,
    local_sem,
    sent_sem,
    agz_sem,
    agx_sem,
    agl_sem,
    agy_sem,
    rsx_sem,
    rsf_sem,
    rsz_sem,
    rcy_sem,
    rcl_sem,
    red_sem,
):
    nzh, nx, nc = rparts
    ny, nzl = cparts
    nrow, ncol = nzh * nx * nc, ny * nzl
    slots = tile_hbm.shape[0]
    coupling = 1.0 / (2.0 * math.sqrt(TILE * (2 * COUPLED + 1)))

    row = lax.axis_index("row")
    col = lax.axis_index("col")
    zh, x, core = row // (nx * nc), row // nc % nx, row % nc
    y, zl = col // nzl, col % nzl

    def row_at(dz, dx, dc):
        return (
            lax.rem(zh + dz, nzh) * (nx * nc)
            + lax.rem(x + dx, nx) * nc
            + lax.rem(core + dc, nc)
        )

    def col_at(dy, dl):
        return lax.rem(y + dy, ny) * nzl + lax.rem(zl + dl, nzl)

    def row_from(dz, dx, dc):
        return row_at(nzh - dz, nx - dx, nc - dc)

    def col_from(dy, dl):
        return col_at(ny - dy, nzl - dl)

    plane = [(dx, dc) for dx in range(nx) for dc in range(nc) if dx or dc]
    plane = sorted(plane, key=lambda p: -min(p[0], nx - p[0]))
    line = [(dz, dl) for dz in range(nzh) for dl in range(nzl) if dz or dl]
    line = sorted(line, key=lambda p: -min(p[0] * nzl + p[1], nzh * nzl - p[0] * nzl - p[1]))
    ys, ls = near_first(ny), list(range(1, nzl))
    near = sorted({1, nzh - 1} - {0})
    far = 2 if nzh == 4 else None
    groups = [0, *near] + ([far] if far else [])

    barrier = pltpu.get_barrier_semaphore()
    peers = [(row_at(d, 0, 0), col) for d in near]
    peers += [(row, col_at(0, d)) for d in ls]
    peers += [(row_at(0, dx, dc), col) for dx, dc in plane]
    peers += [(row, col_at(dy, 0)) for dy in ys]
    for peer in peers:
        pl.semaphore_signal(barrier, inc=1, device_id=peer, device_id_type=MESH)

    def remote(src, dst, kind, sem, device):
        return pltpu.make_async_remote_copy(
            src_ref=src,
            dst_ref=dst,
            send_sem=sent_sem.at[kind],
            recv_sem=sem,
            device_id=device,
            device_id_type=MESH,
        )

    def send(src, dst, kind, sem, device):
        remote(src, dst, kind, sem, device).start()

    def arrive(dst, sem):
        remote(dst, dst, 0, sem, (row, col)).wait_recv()

    def sent(src, kind):
        remote(src, src, kind, agz_sem.at[0, 0], (row, col)).wait_send()

    inputs = (
        (rs_hbm, rs_ref),
        (obs_hbm, obs_ref),
        (noise_hbm, noise_ref),
        (rows_hbm, rows_s),
        (cols_hbm, cols_s),
        (count_hbm, count_s),
        (diag_hbm, diag),
        (tile_hbm, tiles),
    )
    inputs = [
        pltpu.make_async_copy(src, dst, local_sem.at[k])
        for k, (src, dst) in enumerate(inputs)
    ]
    for copy in inputs:
        copy.start()
    for copy in inputs[:6]:
        copy.wait()

    observed = [obs_ref[:, k * TILE : (k + 1) * TILE].astype(F32) for k in range(2)]
    noise = [noise_ref[:, k * TILE : (k + 1) * TILE] for k in range(2)]
    right = [rs_ref[:, k * TILE : (k + 1) * TILE] for k in range(2)]

    def chunk_row(it, r):
        return rowbuf.at[it, pl.ds(2 * r, 2)]

    def chunk_col(it, c):
        return colbuf.at[it, pl.ds(2 * c, 2)]

    def put_masked(it, masked):
        for k in range(2):
            rowbuf[it, 2 * row + k] = masked[k]
            colbuf[it, 2 * col + k] = masked[k]

    def start_gather(it):
        mine_r, mine_c = chunk_row(it, row), chunk_col(it, col)
        for n, d in enumerate(near):
            send(mine_r, mine_r, 0, agz_sem.at[it, n], (row_at(d, 0, 0), col))
        for d in ls:
            send(mine_c, mine_c, 1, agl_sem.at[it, d - 1], (row, col_at(0, d)))
        for d in ys:
            send(mine_c, mine_c, 2, agy_sem.at[it], (row, col_at(d, 0)))
        for dx, dc in plane:
            send(mine_r, mine_r, 3, agx_sem.at[it], (row_at(0, dx, dc), col))

    def col_forward(it, d):
        got = chunk_col(it, col_from(0, d))
        arrive(got, agl_sem.at[it, d - 1])
        for dy in ys:
            send(got, got, 2, agy_sem.at[it], (row, col_at(dy, 0)))

    def to_plane(it, got):
        for dx, dc in plane:
            send(got, got, 3, agx_sem.at[it], (row_at(0, dx, dc), col))

    def near_arrive(it):
        for n, d in enumerate(near):
            r = row_from(d, 0, 0)
            arrive(chunk_row(it, r), agz_sem.at[it, n])
            if far:
                half = rowbuf.at[it, 2 * r + n]
                send(half, half, 0, agz_sem.at[it, 2], (row_at(d, 0, 0), col))

    def near_forward(it):
        for d in near:
            to_plane(it, chunk_row(it, row_from(d, 0, 0)))

    def far_forward(it):
        if far:
            got = chunk_row(it, row_from(far, 0, 0))
            arrive(got, agz_sem.at[it, 2])
            to_plane(it, got)

    def col_done(it):
        arrive(colbuf.at[it, : 2 * (ny - 1) * nzl], agy_sem.at[it])

    def row_done(it):
        arrive(rowbuf.at[it, : 2 * len(plane) * nzh], agx_sem.at[it])

    def product(hot, value):
        high = value.astype(BF16)
        low = (value - high.astype(F32)).astype(BF16)
        both = jnp.concatenate([high, low], axis=1)
        sums = jnp.dot(hot, both, preferred_element_type=F32)
        return sums[:, :TILE] + sums[:, TILE:]

    def terms(picks, pieces, contract):
        for t in range(slots):
            gath[t] = pieces[picks[t]]
        out = lax.dot_general(
            gath[...],
            tiles[...],
            (((2,), (contract,)), ((0,), (0,))),
            preferred_element_type=F32,
        )
        return (out[:, :NRHS] + out[:, NRHS:]).reshape(slots * NRHS, TILE)

    def upper(it):
        for j in range(2 * ncol):
            colsplit[j] = split_rows(colbuf[it, j])
        value = terms(cols_s, colsplit, 2)
        rowterm[it] = product(hrow[...], value).reshape(2 * nrow, NRHS, TILE)
        for dz in reversed(groups):
            for p, (dx, dc) in enumerate(plane):
                send(
                    rowterm.at[it, pl.ds(2 * row_at(dz, dx, dc), 2)],
                    xrecv.at[it, dz, p],
                    4,
                    rsx_sem.at[it, dz],
                    (row_at(0, dx, dc), col),
                )

    def lower(it):
        for i in range(2 * nrow):
            rowsplit[i] = split_rows(rowbuf[it, i])
        value = terms(rows_s, rowsplit, 1)
        colterm[it] = product(hcol[...], value).reshape(2 * ncol, NRHS, TILE)
        for dl in [*ls, 0]:
            for dy in ys:
                send(
                    colterm.at[it, pl.ds(2 * col_at(dy, dl), 2)],
                    yrecv.at[it, dl, dy - 1],
                    5,
                    rcy_sem.at[it, dl],
                    (row, col_at(dy, 0)),
                )

    def plane_sum(it, dz):
        arrive(xrecv.at[it, dz], rsx_sem.at[it, dz])
        total = rowterm[it, pl.ds(2 * row_at(dz, 0, 0), 2)]
        for p in range(len(plane)):
            total = total + xrecv[it, dz, p]
        return total

    def far_reduce(it):
        if far:
            zsend[it, far] = plane_sum(it, far)
            for n, d in enumerate(near):
                send(
                    zsend.at[it, far, n],
                    frecv.at[it, n],
                    6,
                    rsf_sem.at[it, n],
                    (row_at(d, 0, 0), col),
                )

    def near_reduce(it):
        sums = [plane_sum(it, d) for d in near]
        for n, d in enumerate(near):
            zsend[it, d] = sums[n]
            if far:
                arrive(frecv.at[it, n], rsf_sem.at[it, n])
                zsend[it, d, n] = sums[n][n] + frecv[it, n]
            send(zsend.at[it, d], zrecv.at[it, n], 6, rsz_sem.at[it], (row_at(d, 0, 0), col))

    def col_reduce(it, dl):
        arrive(yrecv.at[it, dl], rcy_sem.at[it, dl])
        total = colterm[it, pl.ds(2 * col_at(0, dl), 2)]
        for dy in ys:
            total = total + yrecv[it, dl, dy - 1]
        lsend[it, dl] = total
        if dl:
            send(
                lsend.at[it, dl], lrecv.at[it, dl - 1], 7, rcl_sem.at[it], (row, col_at(0, dl))
            )

    def row_final(it):
        total = plane_sum(it, 0)
        arrive(zrecv.at[it], rsz_sem.at[it])
        for n in range(len(near)):
            total = total + zrecv[it, n]
        return total

    def col_final(it):
        total = lsend[it, 0]
        arrive(lrecv.at[it], rcl_sem.at[it])
        for d in ls:
            total = total + lrecv[it, d - 1]
        return total

    lane = lax.broadcasted_iota(jnp.int32, (NRHS, TILE), 1)
    sub = lax.broadcasted_iota(jnp.int32, (NRHS, TILE), 0)
    stages = (
        [(row_at(0, dx, dc), col) for dx, dc in plane],
        [(row, col_at(dy, 0)) for dy in ys],
        [(row_at(dz, 0, 0), col_at(0, dl)) for dz, dl in line],
    )
    first_slot = (0, len(plane), len(plane) + len(ys))

    def red_send(r, stage, value):
        red_src[r, stage] = value
        for n, device in enumerate(stages[stage]):
            send(
                red_src.at[r, stage],
                red_dst.at[r, first_slot[stage] + n],
                8,
                red_sem.at[r, stage],
                device,
            )

    def red_get(r, stage):
        count = len(stages[stage])
        arrive(red_dst.at[r, pl.ds(first_slot[stage], count)], red_sem.at[r, stage])
        total = red_src[r, stage]
        for n in range(count):
            total = total + red_dst[r, first_slot[stage] + n]
        return total

    def pack(values):
        packed = jnp.zeros((NRHS, TILE), F32)
        for k, value in enumerate(values):
            whole = jnp.sum(value, axis=1, keepdims=True)
            packed = packed + jnp.where(lane == sub + NRHS * k, whole, 0.0)
        return jnp.sum(packed, axis=0, keepdims=True)

    def unpack(total, k):
        return jnp.sum(jnp.where(lane == sub + NRHS * k, total, 0.0), axis=1, keepdims=True)

    masked_b = [observed[k] * right[k] for k in range(2)]
    put_masked(0, masked_b)

    def hot_matrices():
        wide = lax.broadcasted_iota(jnp.int32, (1, slots * NRHS), 1)
        row_index = jnp.zeros((1, slots * NRHS), jnp.int32)
        col_index = jnp.zeros((1, slots * NRHS), jnp.int32)
        for t in range(slots):
            here = wide // NRHS == t
            row_index = jnp.where(here, rows_s[t] * NRHS, row_index)
            col_index = jnp.where(here, cols_s[t] * NRHS, col_index)
        live = wide // NRHS < count_s[0, 0]
        row_index = jnp.where(live, row_index + wide % NRHS, -1)
        col_index = jnp.where(live, col_index + wide % NRHS, -1)
        step = 64
        for ref, index in ((hrow, row_index), (hcol, col_index)):
            for start in range(0, ref.shape[0], step):
                at = lax.broadcasted_iota(jnp.int32, (step, slots * NRHS), 0) + start
                ref[start : start + step] = jnp.where(at == index, 1.0, 0.0).astype(BF16)

    def own_terms(masked):
        out = []
        for k in range(2):
            both = jnp.dot(split_rows(masked[k]), sym[k], preferred_element_type=F32)
            out.append(both[:NRHS] + both[NRHS:])
        return out

    hot_matrices()
    inputs[6].wait()
    a_index = lax.broadcasted_iota(jnp.int32, (TILE, TILE), 0)
    b_index = lax.broadcasted_iota(jnp.int32, (TILE, TILE), 1)
    for k in range(2):
        block = diag[k].astype(F32)
        sym[k] = jnp.where(b_index >= a_index, block, block.T).astype(BF16)
    diag_b = own_terms(masked_b)
    inputs[7].wait()

    pl.semaphore_wait(barrier, len(peers))

    def gather_upper(it):
        for d in ls:
            col_forward(it, d)
        near_arrive(it)
        near_forward(it)

    start_gather(0)
    gather_upper(0)
    col_done(0)
    upper(0)
    far_forward(0)
    row_done(0)
    quad = jnp.zeros((NRHS, TILE), F32)
    for i in range(2 * nrow):
        quad = quad + rowterm[0, i] * rowbuf[0, i]
    quad = 2.0 * quad
    for k in range(2):
        quad = quad + masked_b[k] * diag_b[k]
    quad = coupling * quad
    for k in range(2):
        quad = quad + noise[k] * right[k] * right[k]
    red_send(0, 0, pack([right[0] * right[0] + right[1] * right[1], quad]))
    lower(0)
    far_reduce(0)
    near_reduce(0)
    red_send(0, 1, red_get(0, 0))
    for d in [*ls, 0]:
        col_reduce(0, d)
    mirrored = col_final(0)
    red_send(0, 2, red_get(0, 1))
    total = row_final(0) + mirrored
    w = [
        noise[k] * right[k] + observed[k] * (coupling * (total[k] + diag_b[k]))
        for k in range(2)
    ]

    masked_w = [observed[k] * w[k] for k in range(2)]
    put_masked(1, masked_w)
    start_gather(1)
    diag_w = own_terms(masked_w)
    gather_upper(1)
    first = red_get(0, 2)
    rr0, dad0 = unpack(first, 0), unpack(first, 1)
    alpha = rr0 / dad0
    res = [right[k] - alpha * w[k] for k in range(2)]
    red_send(
        1, 0, pack([res[0] * res[0] + res[1] * res[1], res[0] * w[0] + res[1] * w[1]])
    )
    col_done(1)
    upper(1)
    far_forward(1)
    red_send(1, 1, red_get(1, 0))
    row_done(1)
    quad = jnp.zeros((NRHS, TILE), F32)
    for i in range(2 * nrow):
        quad = quad + (rowterm[0, i] - alpha * rowterm[1, i]) * (
            rowbuf[0, i] - alpha * rowbuf[1, i]
        )
    quad = 2.0 * quad
    for k in range(2):
        quad = quad + (masked_b[k] - alpha * masked_w[k]) * (diag_b[k] - alpha * diag_w[k])
    quad = coupling * quad
    for k in range(2):
        quad = quad + noise[k] * res[k] * res[k]
    red_send(2, 0, pack([quad]))
    lower(1)
    red_send(1, 2, red_get(1, 1))
    far_reduce(1)
    red_send(2, 1, red_get(2, 0))
    near_reduce(1)
    for d in [*ls, 0]:
        col_reduce(1, d)
    red_send(2, 2, red_get(2, 1))
    mirrored = col_final(1)
    total = row_final(1) + mirrored
    second = red_get(1, 2)
    rr1, rw1 = unpack(second, 0), unpack(second, 1)
    beta = rr1 / rr0
    u = [
        noise[k] * w[k] + observed[k] * (coupling * (total[k] + diag_w[k]))
        for k in range(2)
    ]
    third = unpack(red_get(2, 2), 0)
    dad1 = third + 2.0 * beta * rw1 + beta * beta * dad0
    alpha1 = rr1 / dad1
    for k in range(2):
        here = slice(k * TILE, (k + 1) * TILE)
        direction = res[k] + beta * right[k]
        image = (w[k] - alpha * u[k]) + beta * w[k]
        sol_ref[:, here] = alpha * right[k] + alpha1 * direction
        res_ref[:, here] = res[k] - alpha1 * image

    hops = len(near) * 2 if not far else 2 * (len(near) + 1)
    sent(rowbuf.at[0, : 2 * hops], 0)
    sent(rowbuf.at[0, : 4 * len(ls)], 1)
    sent(rowbuf.at[:, : 2 * (ny - 1) * nzl], 2)
    sent(rowbuf.at[:, : 2 * len(plane) * nzh], 3)
    sent(rowbuf.at[:, : 2 * len(plane) * nzh], 4)
    sent(rowbuf.at[:, : 2 * (ny - 1) * nzl], 5)
    sent(rowbuf.at[0, : 2 * hops], 6)
    sent(rowbuf.at[0, : 4 * len(ls)], 7)
    sent(red_dst, 8)


def local(
    rparts,
    cparts,
    right_sides,
    noise_var,
    observed,
    tile_data,
    diag_tiles,
    tile_rows,
    tile_cols,
    tile_count,
):
    slots = tile_data.shape[2]
    nzh, nx, nc = rparts
    ny, nzl = cparts
    nrow, ncol = nzh * nx * nc, ny * nzl
    plane, near = nx * nc - 1, min(2, nzh - 1)
    vmem = pl.BlockSpec(memory_space=pltpu.VMEM)
    hbm = pl.BlockSpec(memory_space=pl.ANY)
    dma = pltpu.SemaphoreType.DMA
    chunk = (2, NRHS, TILE)
    shape = jax.ShapeDtypeStruct(right_sides.shape, F32)
    return pl.pallas_call(
        functools.partial(kernel, rparts, cparts),
        out_shape=(shape, shape),
        in_specs=[hbm] * 8,
        out_specs=(vmem, vmem),
        scratch_shapes=[
            pltpu.VMEM(right_sides.shape, F32),
            pltpu.VMEM((1, 2 * TILE), F32),
            pltpu.VMEM((1, 2 * TILE), jnp.int32),
            pltpu.SMEM((slots,), jnp.int32),
            pltpu.SMEM((slots,), jnp.int32),
            pltpu.SMEM((1, 1), jnp.int32),
            pltpu.VMEM((slots, TILE, TILE), BF16),
            pltpu.VMEM((2, TILE, TILE), BF16),
            pltpu.VMEM((2, TILE, TILE), BF16),
            pltpu.VMEM((2 * nrow * NRHS, slots * NRHS), BF16),
            pltpu.VMEM((2 * ncol * NRHS, slots * NRHS), BF16),
            pltpu.VMEM((2, 2 * nrow, NRHS, TILE), F32),
            pltpu.VMEM((2, 2 * ncol, NRHS, TILE), F32),
            pltpu.VMEM((2 * nrow, 2 * NRHS, TILE), BF16),
            pltpu.VMEM((2 * ncol, 2 * NRHS, TILE), BF16),
            pltpu.VMEM((slots, 2 * NRHS, TILE), BF16),
            pltpu.VMEM((2, 2 * nrow, NRHS, TILE), F32),
            pltpu.VMEM((2, 2 * ncol, NRHS, TILE), F32),
            pltpu.VMEM((2, nzh, plane, *chunk), F32),
            pltpu.VMEM((2, nzh, *chunk), F32),
            pltpu.VMEM((2, 2, NRHS, TILE), F32),
            pltpu.VMEM((2, near, *chunk), F32),
            pltpu.VMEM((2, nzl, ny - 1, *chunk), F32),
            pltpu.VMEM((2, nzl, *chunk), F32),
            pltpu.VMEM((2, nzl - 1, *chunk), F32),
            pltpu.VMEM((3, 3, 1, TILE), F32),
            pltpu.VMEM((3, plane + ny - 1 + nzh * nzl - 1, 1, TILE), F32),
            dma((8,)),
            dma((9,)),
            dma((2, 3)),
            dma((2,)),
            dma((2, nzl - 1)),
            dma((2,)),
            dma((2, nzh)),
            dma((2, 2)),
            dma((2,)),
            dma((2, nzl)),
            dma((2,)),
            dma((3, 3)),
        ],
        compiler_params=pltpu.CompilerParams(
            collective_id=0, has_side_effects=True, vmem_limit_bytes=67043328
        ),
        name="solve",
    )(
        right_sides,
        noise_var.reshape(1, -1),
        observed.reshape(1, -1),
        diag_tiles,
        tile_data.reshape(slots, TILE, TILE),
        tile_rows.reshape(slots),
        tile_cols.reshape(slots),
        tile_count,
    )


def solution(mesh):
    return jax.shard_map(
        functools.partial(local, ROW_PARTS, COL_PARTS),
        mesh=mesh,
        in_specs=(
            P(None, ("row", "col")),
            P(("row", "col")),
            P(("row", "col")),
            P("row", "col", None, None, None),
            P(("row", "col"), None, None),
            P("row", "col", None),
            P("row", "col", None),
            P("row", "col"),
        ),
        out_specs=(P(None, ("row", "col")), P(None, ("row", "col"))),
        check_vma=False,
    )
```

```python
import functools
import math

import jax
import jax.numpy as jnp
from jax import lax
from jax.experimental import pallas as pl
from jax.experimental.pallas import tpu as pltpu
from jax.sharding import PartitionSpec as P

TILE = 128
COUPLED = 32
NRHS = 8
MESH = pl.DeviceIdType.MESH
ROW_PARTS = (4, 4, 2)
COL_PARTS = (4, 4)
F32 = jnp.float32
BF16 = jnp.bfloat16


def split_rows(value):
    high = value.astype(BF16).astype(F32)
    return jnp.concatenate([high, value - high], axis=0).astype(BF16)


def near_first(size):
    return sorted(range(1, size), key=lambda d: min(d, size - d))


def kernel(
    rparts,
    cparts,
    rs_hbm,
    noise_hbm,
    obs_hbm,
    diag_hbm,
    tile_hbm,
    rows_hbm,
    cols_hbm,
    count_hbm,
    sol_ref,
    res_ref,
    rs_ref,
    noise_ref,
    obs_ref,
    rows_s,
    cols_s,
    count_s,
    tiles,
    diag,
    sym,
    hrow,
    hcol,
    rowbuf,
    colbuf,
    rowsplit,
    colsplit,
    gath,
    rowterm,
    colterm,
    xrecv,
    psum,
    zrecv,
    yrecv,
    lsend,
    lrecv,
    red_src,
    red_dst,
    local_sem,
    sent_sem,
    agz_sem,
    agx_sem,
    agl_sem,
    agy_sem,
    rsx_sem,
    rsz_sem,
    rcy_sem,
    rcl_sem,
    red_sem,
):
    nzh, nx, nc = rparts
    ny, nzl = cparts
    nrow, ncol = nzh * nx * nc, ny * nzl
    slots = tile_hbm.shape[0]
    coupling = 1.0 / (2.0 * math.sqrt(TILE * (2 * COUPLED + 1)))

    row = lax.axis_index("row")
    col = lax.axis_index("col")
    zh, x, core = row // (nx * nc), row // nc % nx, row % nc
    y, zl = col // nzl, col % nzl

    def row_at(dz, dx, dc):
        return (
            lax.rem(zh + dz, nzh) * (nx * nc)
            + lax.rem(x + dx, nx) * nc
            + lax.rem(core + dc, nc)
        )

    def col_at(dy, dl):
        return lax.rem(y + dy, ny) * nzl + lax.rem(zl + dl, nzl)

    def row_from(dz, dx, dc):
        return row_at(nzh - dz, nx - dx, nc - dc)

    def col_from(dy, dl):
        return col_at(ny - dy, nzl - dl)

    plane = [(dx, dc) for dx in range(nx) for dc in range(nc) if dx or dc]
    plane = sorted(plane, key=lambda p: -min(p[0], nx - p[0]))
    line = [(dz, dl) for dz in range(nzh) for dl in range(nzl) if dz or dl]
    line = sorted(line, key=lambda p: -min(p[0] * nzl + p[1], nzh * nzl - p[0] * nzl - p[1]))
    ys, ls = near_first(ny), list(range(1, nzl))
    near = sorted({1, nzh - 1} - {0})
    far = 2 if nzh == 4 else None
    groups = [0, *near] + ([far] if far else [])

    barrier = pltpu.get_barrier_semaphore()
    peers = [(row_at(d, 0, 0), col) for d in near]
    peers += [(row, col_at(0, d)) for d in ls]
    peers += [(row_at(0, dx, dc), col) for dx, dc in plane]
    peers += [(row, col_at(dy, 0)) for dy in ys]
    for peer in peers:
        pl.semaphore_signal(barrier, inc=1, device_id=peer, device_id_type=MESH)

    def remote(src, dst, kind, sem, device):
        return pltpu.make_async_remote_copy(
            src_ref=src,
            dst_ref=dst,
            send_sem=sent_sem.at[kind],
            recv_sem=sem,
            device_id=device,
            device_id_type=MESH,
        )

    def send(src, dst, kind, sem, device):
        remote(src, dst, kind, sem, device).start()

    def arrive(dst, sem):
        remote(dst, dst, 0, sem, (row, col)).wait_recv()

    def sent(src, kind):
        remote(src, src, kind, agz_sem.at[0, 0], (row, col)).wait_send()

    inputs = (
        (rs_hbm, rs_ref),
        (obs_hbm, obs_ref),
        (noise_hbm, noise_ref),
        (rows_hbm, rows_s),
        (cols_hbm, cols_s),
        (count_hbm, count_s),
        (diag_hbm, diag),
        (tile_hbm, tiles),
    )
    inputs = [
        pltpu.make_async_copy(src, dst, local_sem.at[k])
        for k, (src, dst) in enumerate(inputs)
    ]
    for copy in inputs:
        copy.start()
    for copy in inputs[:6]:
        copy.wait()

    observed = [obs_ref[:, k * TILE : (k + 1) * TILE].astype(F32) for k in range(2)]
    noise = [noise_ref[:, k * TILE : (k + 1) * TILE] for k in range(2)]
    right = [rs_ref[:, k * TILE : (k + 1) * TILE] for k in range(2)]

    def chunk_row(it, r):
        return rowbuf.at[it, pl.ds(2 * r, 2)]

    def chunk_col(it, c):
        return colbuf.at[it, pl.ds(2 * c, 2)]

    def put_masked(it, masked):
        for k in range(2):
            rowbuf[it, 2 * row + k] = masked[k]
            colbuf[it, 2 * col + k] = masked[k]

    def start_gather(it):
        mine_r, mine_c = chunk_row(it, row), chunk_col(it, col)
        for d in reversed(ls):
            send(mine_c, mine_c, 1, agl_sem.at[it, d - 1], (row, col_at(0, d)))
        if far and it:
            send(mine_r, mine_r, 0, agz_sem.at[it, 2], (row_at(far, 0, 0), col))
        for n, d in enumerate(near):
            send(mine_r, mine_r, 0, agz_sem.at[it, n], (row_at(d, 0, 0), col))
        for d in ys:
            send(mine_c, mine_c, 2, agy_sem.at[it], (row, col_at(d, 0)))
        for dx, dc in plane:
            send(mine_r, mine_r, 3, agx_sem.at[it], (row_at(0, dx, dc), col))

    def col_forward(it, d):
        got = chunk_col(it, col_from(0, d))
        arrive(got, agl_sem.at[it, d - 1])
        for dy in ys:
            send(got, got, 2, agy_sem.at[it], (row, col_at(dy, 0)))

    def to_plane(it, got):
        for dx, dc in plane:
            send(got, got, 3, agx_sem.at[it], (row_at(0, dx, dc), col))

    def near_arrive(it):
        for n, d in enumerate(near):
            r = row_from(d, 0, 0)
            arrive(chunk_row(it, r), agz_sem.at[it, n])
            if far and not it:
                half = rowbuf.at[it, 2 * r + n]
                send(half, half, 0, agz_sem.at[it, 2], (row_at(d, 0, 0), col))

    def near_forward(it):
        for d in near:
            to_plane(it, chunk_row(it, row_from(d, 0, 0)))

    def far_forward(it):
        if far:
            got = chunk_row(it, row_from(far, 0, 0))
            arrive(got, agz_sem.at[it, 2])
            to_plane(it, got)

    def col_done(it):
        arrive(colbuf.at[it, : 2 * (ny - 1) * nzl], agy_sem.at[it])

    def row_done(it):
        arrive(rowbuf.at[it, : 2 * len(plane) * nzh], agx_sem.at[it])

    def product(hot, value):
        high = value.astype(BF16)
        low = (value - high.astype(F32)).astype(BF16)
        both = jnp.concatenate([high, low], axis=1)
        sums = jnp.dot(hot, both, preferred_element_type=F32)
        return sums[:, :TILE] + sums[:, TILE:]

    def terms(picks, pieces, contract):
        for t in range(slots):
            gath[t] = pieces[picks[t]]
        out = lax.dot_general(
            gath[...],
            tiles[...],
            (((2,), (contract,)), ((0,), (0,))),
            preferred_element_type=F32,
        )
        return (out[:, :NRHS] + out[:, NRHS:]).reshape(slots * NRHS, TILE)

    def upper(it):
        for j in range(2 * ncol):
            colsplit[j] = split_rows(colbuf[it, j])
        value = terms(cols_s, colsplit, 2)
        rowterm[it] = product(hrow[...], value).reshape(2 * nrow, NRHS, TILE)

    def to_rows(it, which):
        for dz in which:
            for p, (dx, dc) in enumerate(plane):
                send(
                    rowterm.at[it, pl.ds(2 * row_at(dz, dx, dc), 2)],
                    xrecv.at[it, dz, p],
                    4,
                    rsx_sem.at[it, dz],
                    (row_at(0, dx, dc), col),
                )

    def lower(it):
        for i in range(2 * nrow):
            rowsplit[i] = split_rows(rowbuf[it, i])
        value = terms(rows_s, rowsplit, 1)
        colterm[it] = product(hcol[...], value).reshape(2 * ncol, NRHS, TILE)
        for dl in [*ls, 0]:
            for dy in ys:
                send(
                    colterm.at[it, pl.ds(2 * col_at(dy, dl), 2)],
                    yrecv.at[it, dl, dy - 1],
                    5,
                    rcy_sem.at[it, dl],
                    (row, col_at(dy, 0)),
                )

    def plane_sum(it, dz):
        arrive(xrecv.at[it, dz], rsx_sem.at[it, dz])
        total = rowterm[it, pl.ds(2 * row_at(dz, 0, 0), 2)]
        for p in range(len(plane)):
            total = total + xrecv[it, dz, p]
        psum[it, dz] = total
        if dz:
            send(psum.at[it, dz], zrecv.at[it, dz - 1], 6, rsz_sem.at[it], (row_at(dz, 0, 0), col))

    def col_reduce(it, dl):
        arrive(yrecv.at[it, dl], rcy_sem.at[it, dl])
        total = colterm[it, pl.ds(2 * col_at(0, dl), 2)]
        for dy in ys:
            total = total + yrecv[it, dl, dy - 1]
        lsend[it, dl] = total
        if dl:
            send(
                lsend.at[it, dl], lrecv.at[it, dl - 1], 7, rcl_sem.at[it], (row, col_at(0, dl))
            )

    def row_final(it):
        total = psum[it, 0]
        arrive(zrecv.at[it], rsz_sem.at[it])
        for d in range(nzh - 1):
            total = total + zrecv[it, d]
        return total

    def col_final(it):
        total = lsend[it, 0]
        arrive(lrecv.at[it], rcl_sem.at[it])
        for d in ls:
            total = total + lrecv[it, d - 1]
        return total

    lane = lax.broadcasted_iota(jnp.int32, (NRHS, TILE), 1)
    sub = lax.broadcasted_iota(jnp.int32, (NRHS, TILE), 0)
    slab = [(dx, dc, dy) for dx, dc in [*plane, (0, 0)] for dy in [*reversed(ys), 0]]
    stages = (
        [(row_at(0, dx, dc), col_at(dy, 0)) for dx, dc, dy in slab[:-1]],
        [(row_at(dz, 0, 0), col_at(0, dl)) for dz, dl in line],
    )
    first_slot = (0, len(slab) - 1)

    def red_send(r, stage, value):
        red_src[r, stage] = value
        for n, device in enumerate(stages[stage]):
            send(
                red_src.at[r, stage],
                red_dst.at[r, first_slot[stage] + n],
                8,
                red_sem.at[r, stage],
                device,
            )

    def red_get(r, stage):
        count = len(stages[stage])
        arrive(red_dst.at[r, pl.ds(first_slot[stage], count)], red_sem.at[r, stage])
        total = red_src[r, stage]
        for n in range(count):
            total = total + red_dst[r, first_slot[stage] + n]
        return total

    def pack(values):
        packed = jnp.zeros((NRHS, TILE), F32)
        for k, value in enumerate(values):
            whole = jnp.sum(value, axis=1, keepdims=True)
            packed = packed + jnp.where(lane == sub + NRHS * k, whole, 0.0)
        return jnp.sum(packed, axis=0, keepdims=True)

    def unpack(total, k):
        return jnp.sum(jnp.where(lane == sub + NRHS * k, total, 0.0), axis=1, keepdims=True)

    masked_b = [observed[k] * right[k] for k in range(2)]
    put_masked(0, masked_b)

    def hot_matrices():
        wide = lax.broadcasted_iota(jnp.int32, (1, slots * NRHS), 1)
        row_index = jnp.zeros((1, slots * NRHS), jnp.int32)
        col_index = jnp.zeros((1, slots * NRHS), jnp.int32)
        for t in range(slots):
            here = wide // NRHS == t
            row_index = jnp.where(here, rows_s[t] * NRHS, row_index)
            col_index = jnp.where(here, cols_s[t] * NRHS, col_index)
        live = wide // NRHS < count_s[0, 0]
        row_index = jnp.where(live, row_index + wide % NRHS, -1)
        col_index = jnp.where(live, col_index + wide % NRHS, -1)
        step = 64
        for ref, index in ((hrow, row_index), (hcol, col_index)):
            for start in range(0, ref.shape[0], step):
                at = lax.broadcasted_iota(jnp.int32, (step, slots * NRHS), 0) + start
                ref[start : start + step] = jnp.where(at == index, 1.0, 0.0).astype(BF16)

    def own_terms(masked):
        out = []
        for k in range(2):
            both = jnp.dot(split_rows(masked[k]), sym[k], preferred_element_type=F32)
            out.append(both[:NRHS] + both[NRHS:])
        return out

    hot_matrices()
    inputs[6].wait()
    a_index = lax.broadcasted_iota(jnp.int32, (TILE, TILE), 0)
    b_index = lax.broadcasted_iota(jnp.int32, (TILE, TILE), 1)
    for k in range(2):
        block = diag[k].astype(F32)
        sym[k] = jnp.where(b_index >= a_index, block, block.T).astype(BF16)
    diag_b = own_terms(masked_b)
    inputs[7].wait()

    pl.semaphore_wait(barrier, len(peers))

    outer = [far] if far else []

    start_gather(0)
    for d in ls:
        col_forward(0, d)
    near_arrive(0)
    near_forward(0)
    col_done(0)
    upper(0)
    to_rows(0, outer)
    far_forward(0)
    to_rows(0, [*near, 0])
    for d in [*outer, *near, 0]:
        plane_sum(0, d)
    row_done(0)
    lower(0)
    quad = jnp.zeros((NRHS, TILE), F32)
    for d in groups:
        for k in range(2):
            quad = quad + psum[0, d, k] * rowbuf[0, 2 * row_at(d, 0, 0) + k]
    quad = 2.0 * quad
    for k in range(2):
        quad = quad + masked_b[k] * diag_b[k]
    quad = coupling * quad
    for k in range(2):
        quad = quad + noise[k] * right[k] * right[k]
    red_send(0, 0, pack([right[0] * right[0] + right[1] * right[1], quad]))
    for d in [*ls, 0]:
        col_reduce(0, d)
    red_send(0, 1, red_get(0, 0))
    total = row_final(0) + col_final(0)
    w = [
        noise[k] * right[k] + observed[k] * (coupling * (total[k] + diag_b[k]))
        for k in range(2)
    ]

    masked_w = [observed[k] * w[k] for k in range(2)]
    put_masked(1, masked_w)
    start_gather(1)
    diag_w = own_terms(masked_w)
    for d in ls:
        col_forward(1, d)
    near_arrive(1)
    near_forward(1)
    col_done(1)
    upper(1)
    to_rows(1, [*outer, *near, 0])
    first = red_get(0, 1)
    rr0, dad0 = unpack(first, 0), unpack(first, 1)
    alpha = rr0 / dad0
    res = [right[k] - alpha * w[k] for k in range(2)]
    red_send(
        1, 0, pack([res[0] * res[0] + res[1] * res[1], res[0] * w[0] + res[1] * w[1]])
    )
    far_forward(1)
    for d in [*outer, *near, 0]:
        plane_sum(1, d)
    quad = jnp.zeros((NRHS, TILE), F32)
    for d in groups:
        for k in range(2):
            block = 2 * row_at(d, 0, 0) + k
            quad = quad + (psum[0, d, k] - alpha * psum[1, d, k]) * (
                rowbuf[0, block] - alpha * rowbuf[1, block]
            )
    quad = 2.0 * quad
    for k in range(2):
        quad = quad + (masked_b[k] - alpha * masked_w[k]) * (diag_b[k] - alpha * diag_w[k])
    quad = coupling * quad
    for k in range(2):
        quad = quad + noise[k] * res[k] * res[k]
    red_send(2, 0, pack([quad]))
    red_send(1, 1, red_get(1, 0))
    row_done(1)
    lower(1)
    red_send(2, 1, red_get(2, 0))
    for d in [*ls, 0]:
        col_reduce(1, d)
    total = row_final(1) + col_final(1)
    second = red_get(1, 1)
    rr1, rw1 = unpack(second, 0), unpack(second, 1)
    beta = rr1 / rr0
    u = [
        noise[k] * w[k] + observed[k] * (coupling * (total[k] + diag_w[k]))
        for k in range(2)
    ]
    third = unpack(red_get(2, 1), 0)
    dad1 = third + 2.0 * beta * rw1 + beta * beta * dad0
    alpha1 = rr1 / dad1
    for k in range(2):
        here = slice(k * TILE, (k + 1) * TILE)
        direction = res[k] + beta * right[k]
        image = (w[k] - alpha * u[k]) + beta * w[k]
        sol_ref[:, here] = alpha * right[k] + alpha1 * direction
        res_ref[:, here] = res[k] - alpha1 * image

    hops = 2 * (nzh - 1)
    sent(rowbuf.at[0, : 2 * hops], 0)
    sent(rowbuf.at[0, : 4 * len(ls)], 1)
    sent(rowbuf.at[:, : 2 * (ny - 1) * nzl], 2)
    sent(rowbuf.at[:, : 2 * len(plane) * nzh], 3)
    sent(rowbuf.at[:, : 2 * len(plane) * nzh], 4)
    sent(rowbuf.at[:, : 2 * (ny - 1) * nzl], 5)
    sent(rowbuf.at[0, : 2 * hops], 6)
    sent(rowbuf.at[0, : 4 * len(ls)], 7)
    sent(red_dst, 8)


def local(
    rparts,
    cparts,
    right_sides,
    noise_var,
    observed,
    tile_data,
    diag_tiles,
    tile_rows,
    tile_cols,
    tile_count,
):
    slots = tile_data.shape[2]
    nzh, nx, nc = rparts
    ny, nzl = cparts
    nrow, ncol = nzh * nx * nc, ny * nzl
    plane = nx * nc - 1
    vmem = pl.BlockSpec(memory_space=pltpu.VMEM)
    hbm = pl.BlockSpec(memory_space=pltpu.HBM)
    dma = pltpu.SemaphoreType.DMA
    chunk = (2, NRHS, TILE)
    shape = jax.ShapeDtypeStruct(right_sides.shape, F32)
    return pl.pallas_call(
        functools.partial(kernel, rparts, cparts),
        out_shape=(shape, shape),
        in_specs=[hbm] * 8,
        out_specs=(vmem, vmem),
        scratch_shapes=[
            pltpu.VMEM(right_sides.shape, F32),
            pltpu.VMEM((1, 2 * TILE), F32),
            pltpu.VMEM((1, 2 * TILE), jnp.int32),
            pltpu.SMEM((slots,), jnp.int32),
            pltpu.SMEM((slots,), jnp.int32),
            pltpu.SMEM((1, 1), jnp.int32),
            pltpu.VMEM((slots, TILE, TILE), BF16),
            pltpu.VMEM((2, TILE, TILE), BF16),
            pltpu.VMEM((2, TILE, TILE), BF16),
            pltpu.VMEM((2 * nrow * NRHS, slots * NRHS), BF16),
            pltpu.VMEM((2 * ncol * NRHS, slots * NRHS), BF16),
            pltpu.VMEM((2, 2 * nrow, NRHS, TILE), F32),
            pltpu.VMEM((2, 2 * ncol, NRHS, TILE), F32),
            pltpu.VMEM((2 * nrow, 2 * NRHS, TILE), BF16),
            pltpu.VMEM((2 * ncol, 2 * NRHS, TILE), BF16),
            pltpu.VMEM((slots, 2 * NRHS, TILE), BF16),
            pltpu.VMEM((2, 2 * nrow, NRHS, TILE), F32),
            pltpu.VMEM((2, 2 * ncol, NRHS, TILE), F32),
            pltpu.VMEM((2, nzh, plane, *chunk), F32),
            pltpu.VMEM((2, nzh, *chunk), F32),
            pltpu.VMEM((2, nzh - 1, *chunk), F32),
            pltpu.VMEM((2, nzl, ny - 1, *chunk), F32),
            pltpu.VMEM((2, nzl, *chunk), F32),
            pltpu.VMEM((2, nzl - 1, *chunk), F32),
            pltpu.VMEM((3, 2, 1, TILE), F32),
            pltpu.VMEM((3, (plane + 1) * ny - 1 + nzh * nzl - 1, 1, TILE), F32),
            dma((8,)),
            dma((9,)),
            dma((2, 3)),
            dma((2,)),
            dma((2, nzl - 1)),
            dma((2,)),
            dma((2, nzh)),
            dma((2,)),
            dma((2, nzl)),
            dma((2,)),
            dma((3, 2)),
        ],
        compiler_params=pltpu.CompilerParams(
            collective_id=0, has_side_effects=True, vmem_limit_bytes=67043328
        ),
        name="solve",
    )(
        right_sides,
        noise_var.reshape(1, -1),
        observed.reshape(1, -1),
        diag_tiles,
        tile_data.reshape(slots, TILE, TILE),
        tile_rows.reshape(slots),
        tile_cols.reshape(slots),
        tile_count,
    )


def solution(mesh):
    return jax.shard_map(
        functools.partial(local, ROW_PARTS, COL_PARTS),
        mesh=mesh,
        in_specs=(
            P(None, ("row", "col")),
            P(("row", "col")),
            P(("row", "col")),
            P("row", "col", None, None, None),
            P(("row", "col"), None, None),
            P("row", "col", None),
            P("row", "col", None),
            P("row", "col"),
        ),
        out_specs=(P(None, ("row", "col")), P(None, ("row", "col"))),
        check_vma=False,
    )
```

```python
import functools
import math

import jax
import jax.numpy as jnp
from jax import lax
from jax.experimental import pallas as pl
from jax.experimental.pallas import tpu as pltpu
from jax.sharding import PartitionSpec as P

TILE = 128
COUPLED = 32
NRHS = 8
MESH = pl.DeviceIdType.MESH
ROW_PARTS = (4, 4, 2)
COL_PARTS = (4, 4)
F32 = jnp.float32
BF16 = jnp.bfloat16


def split_rows(value):
    high = value.astype(BF16).astype(F32)
    return jnp.concatenate([high, value - high], axis=0).astype(BF16)


def near_first(size):
    return sorted(range(1, size), key=lambda d: min(d, size - d))


def kernel(
    rparts,
    cparts,
    rs_hbm,
    noise_hbm,
    obs_hbm,
    diag_hbm,
    tile_hbm,
    rows_hbm,
    cols_hbm,
    count_hbm,
    sol_ref,
    res_ref,
    rs_ref,
    noise_ref,
    obs_ref,
    rows_s,
    cols_s,
    count_s,
    tiles,
    diag,
    sym,
    hrow,
    hcol,
    rowbuf,
    colbuf,
    rowsplit,
    colsplit,
    both,
    rowterm,
    colterm,
    xrecv,
    psum,
    zrecv,
    yrecv,
    red_src,
    red_dst,
    local_sem,
    sent_sem,
    agz_sem,
    agx_sem,
    agl_sem,
    agy_sem,
    rsx_sem,
    rsz_sem,
    rcy_sem,
    red_sem,
):
    nzh, nx, nc = rparts
    ny, nzl = cparts
    nrow, ncol = nzh * nx * nc, ny * nzl
    slots = tile_hbm.shape[0]
    coupling = 1.0 / (2.0 * math.sqrt(TILE * (2 * COUPLED + 1)))

    row = lax.axis_index("row")
    col = lax.axis_index("col")
    zh, x, core = row // (nx * nc), row // nc % nx, row % nc
    y, zl = col // nzl, col % nzl

    def row_at(dz, dx, dc):
        return (
            lax.rem(zh + dz, nzh) * (nx * nc)
            + lax.rem(x + dx, nx) * nc
            + lax.rem(core + dc, nc)
        )

    def col_at(dy, dl):
        return lax.rem(y + dy, ny) * nzl + lax.rem(zl + dl, nzl)

    def row_from(dz, dx, dc):
        return row_at(nzh - dz, nx - dx, nc - dc)

    def col_from(dy, dl):
        return col_at(ny - dy, nzl - dl)

    plane = [(dx, dc) for dx in range(nx) for dc in range(nc) if dx or dc]
    plane = sorted(plane, key=lambda p: -min(p[0], nx - p[0]))
    line = [(dz, dl) for dz in range(nzh) for dl in range(nzl) if dz or dl]
    line = sorted(line, key=lambda p: -min(p[0] * nzl + p[1], nzh * nzl - p[0] * nzl - p[1]))
    ys, ls = near_first(ny), list(range(1, nzl))
    ring = [(dy, dl) for dy in range(ny) for dl in range(nzl) if dy or dl]
    ring = sorted(ring, key=lambda p: -min(p[0], ny - p[0]) - (2 if p[1] else 0))
    near = sorted({1, nzh - 1} - {0})
    far = 2 if nzh == 4 else None
    inner = [*near, 0]
    outer = [far] if far else []

    barrier = pltpu.get_barrier_semaphore()
    peers = [(row_at(d, 0, 0), col) for d in near]
    peers += [(row, col_at(0, d)) for d in ls]
    peers += [(row_at(0, dx, dc), col) for dx, dc in plane]
    peers += [(row, col_at(dy, 0)) for dy in ys]
    for peer in peers:
        pl.semaphore_signal(barrier, inc=1, device_id=peer, device_id_type=MESH)

    def remote(src, dst, kind, sem, device):
        return pltpu.make_async_remote_copy(
            src_ref=src,
            dst_ref=dst,
            send_sem=sent_sem.at[kind],
            recv_sem=sem,
            device_id=device,
            device_id_type=MESH,
        )

    def send(src, dst, kind, sem, device):
        remote(src, dst, kind, sem, device).start()

    def arrive(dst, sem):
        remote(dst, dst, 0, sem, (row, col)).wait_recv()

    def sent(src, kind):
        remote(src, src, kind, agz_sem.at[0, 0], (row, col)).wait_send()

    inputs = (
        (rs_hbm, rs_ref),
        (obs_hbm, obs_ref),
        (noise_hbm, noise_ref),
        (rows_hbm, rows_s),
        (cols_hbm, cols_s),
        (count_hbm, count_s),
        (diag_hbm, diag),
        (tile_hbm, tiles),
    )
    inputs = [
        pltpu.make_async_copy(src, dst, local_sem.at[k])
        for k, (src, dst) in enumerate(inputs)
    ]
    for copy in inputs:
        copy.start()
    for copy in inputs[:6]:
        copy.wait()

    observed = [obs_ref[:, k * TILE : (k + 1) * TILE].astype(F32) for k in range(2)]
    noise = [noise_ref[:, k * TILE : (k + 1) * TILE] for k in range(2)]
    right = [rs_ref[:, k * TILE : (k + 1) * TILE] for k in range(2)]

    def chunk_row(it, r):
        return rowbuf.at[it, pl.ds(2 * r, 2)]

    def chunk_col(it, c):
        return colbuf.at[it, pl.ds(2 * c, 2)]

    def put_masked(it, masked):
        for k in range(2):
            rowbuf[it, 2 * row + k] = masked[k]
            colbuf[it, 2 * col + k] = masked[k]

    def start_gather(it):
        mine_r, mine_c = chunk_row(it, row), chunk_col(it, col)
        if it:
            for dy, dl in ring:
                send(mine_c, mine_c, 2, agy_sem.at[it], (row, col_at(dy, dl)))
            if far:
                send(mine_r, mine_r, 0, agz_sem.at[it, 2], (row_at(far, 0, 0), col))
        for n, d in enumerate(near):
            send(mine_r, mine_r, 0, agz_sem.at[it, n], (row_at(d, 0, 0), col))
        if not it:
            for d in reversed(ls):
                send(mine_c, mine_c, 1, agl_sem.at[d - 1], (row, col_at(0, d)))
            for d in ys:
                send(mine_c, mine_c, 2, agy_sem.at[it], (row, col_at(d, 0)))
        for dx, dc in plane:
            send(mine_r, mine_r, 3, agx_sem.at[it, 0], (row_at(0, dx, dc), col))

    def col_forward(d):
        got = chunk_col(0, col_from(0, d))
        arrive(got, agl_sem.at[d - 1])
        for dy in ys:
            send(got, got, 2, agy_sem.at[0], (row, col_at(dy, 0)))

    def to_plane(it, got, late):
        for dx, dc in plane:
            send(got, got, 3, agx_sem.at[it, late], (row_at(0, dx, dc), col))

    def near_arrive(it):
        for n, d in enumerate(near):
            r = row_from(d, 0, 0)
            arrive(chunk_row(it, r), agz_sem.at[it, n])
            if far and not it:
                half = rowbuf.at[it, 2 * r + n]
                send(half, half, 0, agz_sem.at[it, 2], (row_at(d, 0, 0), col))

    def near_forward(it):
        for d in near:
            to_plane(it, chunk_row(it, row_from(d, 0, 0)), 0)

    def far_forward(it):
        if far:
            got = chunk_row(it, row_from(far, 0, 0))
            arrive(got, agz_sem.at[it, 2])
            to_plane(it, got, 1)

    def col_done(it):
        count = ncol - 1 if it else (ny - 1) * nzl
        arrive(colbuf.at[it, : 2 * count], agy_sem.at[it])

    def near_done(it):
        arrive(rowbuf.at[it, : 2 * len(plane) * len(inner)], agx_sem.at[it, 0])

    def row_done(it):
        if far:
            arrive(rowbuf.at[it, : 2 * len(plane)], agx_sem.at[it, 1])

    def product(hot):
        sums = jnp.dot(hot, both[...], preferred_element_type=F32)
        return (sums[:, :TILE] + sums[:, TILE:]).reshape(hot.shape[0] // NRHS, NRHS, TILE)

    def terms(picks, pieces, contract):
        for t in range(0, slots, 2):
            left = jnp.concatenate([pieces[picks[t]], pieces[picks[t + 1]]], axis=0)
            if contract:
                pair = tiles[t : t + 2].reshape(2 * TILE, TILE)
            else:
                pair = jnp.concatenate([tiles[t], tiles[t + 1]], axis=1)
            sums = lax.dot_general(
                left, pair, (((1,), (contract,)), ((), ())), preferred_element_type=F32
            )
            value = []
            for k in range(2):
                part = sums[2 * NRHS * k : 2 * NRHS * (k + 1), TILE * k : TILE * (k + 1)]
                value.append(part[:NRHS] + part[NRHS:])
            value = jnp.concatenate(value, axis=0)
            high = value.astype(BF16)
            low = (value - high.astype(F32)).astype(BF16)
            both[t * NRHS : (t + 2) * NRHS] = jnp.concatenate([high, low], axis=1)

    def upper(it):
        for j in range(2 * ncol):
            colsplit[j] = split_rows(colbuf[it, j])
        terms(cols_s, colsplit, 1)

    def row_block(dx, dc):
        return 2 * (lax.rem(x + dx, nx) * nc + lax.rem(core + dc, nc))

    def to_rows(it, which):
        count = 2 * nx * nc * NRHS
        for dz in which:
            rowterm[it, dz] = product(hrow[dz * count : (dz + 1) * count])
        for dz in which:
            for p, (dx, dc) in enumerate(plane):
                send(
                    rowterm.at[it, dz, pl.ds(row_block(dx, dc), 2)],
                    xrecv.at[it, dz, p],
                    4,
                    rsx_sem.at[it, dz],
                    (row_at(0, dx, dc), col),
                )

    def split_chunk(it, r):
        for k in range(2):
            rowsplit[2 * r + k] = split_rows(rowbuf[it, 2 * r + k])

    def split_plane(it, which):
        for d in which:
            for dx in range(nx):
                for dc in range(nc):
                    split_chunk(it, row_at(d, dx, dc))

    def lower(it):
        terms(rows_s, rowsplit, 0)
        colterm[it] = product(hcol[...])
        for n, (dy, dl) in enumerate(ring):
            send(
                colterm.at[it, pl.ds(2 * col_at(dy, dl), 2)],
                yrecv.at[it, n],
                5,
                rcy_sem.at[it],
                (row, col_at(dy, dl)),
            )

    def plane_sum(it, dz):
        arrive(xrecv.at[it, dz], rsx_sem.at[it, dz])
        total = rowterm[it, dz, pl.ds(row_block(0, 0), 2)]
        for p in range(len(plane)):
            total = total + xrecv[it, dz, p]
        psum[it, dz] = total
        if dz:
            send(psum.at[it, dz], zrecv.at[it, dz - 1], 6, rsz_sem.at[it], (row_at(dz, 0, 0), col))

    def row_final(it):
        total = psum[it, 0]
        arrive(zrecv.at[it], rsz_sem.at[it])
        for d in range(nzh - 1):
            total = total + zrecv[it, d]
        return total

    def col_final(it):
        arrive(yrecv.at[it], rcy_sem.at[it])
        total = colterm[it, pl.ds(2 * col, 2)]
        for n in range(ncol - 1):
            total = total + yrecv[it, n]
        return total

    lane = lax.broadcasted_iota(jnp.int32, (NRHS, TILE), 1)
    sub = lax.broadcasted_iota(jnp.int32, (NRHS, TILE), 0)
    slab = [(dx, dc, dy) for dx, dc in [*plane, (0, 0)] for dy in [*reversed(ys), 0]]
    stages = (
        [(row_at(0, dx, dc), col_at(dy, 0)) for dx, dc, dy in slab[:-1]],
        [(row_at(dz, 0, 0), col_at(0, dl)) for dz, dl in line],
    )
    first_slot = (0, len(slab) - 1)

    def red_send(r, stage, value):
        red_src[r, stage] = value
        for n, device in enumerate(stages[stage]):
            send(
                red_src.at[r, stage],
                red_dst.at[r, first_slot[stage] + n],
                7,
                red_sem.at[r, stage],
                device,
            )

    def red_get(r, stage):
        count = len(stages[stage])
        arrive(red_dst.at[r, pl.ds(first_slot[stage], count)], red_sem.at[r, stage])
        total = red_src[r, stage]
        for n in range(count):
            total = total + red_dst[r, first_slot[stage] + n]
        return total

    def pack(values):
        packed = jnp.zeros((NRHS, TILE), F32)
        for k, value in enumerate(values):
            whole = jnp.sum(value, axis=1, keepdims=True)
            packed = packed + jnp.where(lane == sub + NRHS * k, whole, 0.0)
        return jnp.sum(packed, axis=0, keepdims=True)

    def unpack(total, k):
        return jnp.sum(jnp.where(lane == sub + NRHS * k, total, 0.0), axis=1, keepdims=True)

    masked_b = [observed[k] * right[k] for k in range(2)]
    put_masked(0, masked_b)

    def hot_matrices():
        wide = lax.broadcasted_iota(jnp.int32, (1, slots * NRHS), 1)
        row_index = jnp.zeros((1, slots * NRHS), jnp.int32)
        col_index = jnp.zeros((1, slots * NRHS), jnp.int32)
        for t in range(slots):
            here = wide // NRHS == t
            row_index = jnp.where(here, rows_s[t] * NRHS, row_index)
            col_index = jnp.where(here, cols_s[t] * NRHS, col_index)
        here = 2 * nx * nc * NRHS
        row_index = (row_index // here + (nzh - zh)) % nzh * here + row_index % here
        live = wide // NRHS < count_s[0, 0]
        row_index = jnp.where(live, row_index + wide % NRHS, -1)
        col_index = jnp.where(live, col_index + wide % NRHS, -1)
        step = 64
        for ref, index in ((hrow, row_index), (hcol, col_index)):
            for start in range(0, ref.shape[0], step):
                at = lax.broadcasted_iota(jnp.int32, (step, slots * NRHS), 0) + start
                ref[start : start + step] = jnp.where(at == index, 1.0, 0.0).astype(BF16)

    def own_terms(masked):
        out = []
        for k in range(2):
            both = jnp.dot(split_rows(masked[k]), sym[k], preferred_element_type=F32)
            out.append(both[:NRHS] + both[NRHS:])
        return out

    hot_matrices()
    inputs[6].wait()
    a_index = lax.broadcasted_iota(jnp.int32, (TILE, TILE), 0)
    b_index = lax.broadcasted_iota(jnp.int32, (TILE, TILE), 1)
    for k in range(2):
        block = diag[k].astype(F32)
        sym[k] = jnp.where(b_index >= a_index, block, block.T).astype(BF16)
    diag_b = own_terms(masked_b)
    inputs[7].wait()

    pl.semaphore_wait(barrier, len(peers))

    def far_pairs():
        return [((d, k), 2 * row_at(d, 0, 0) + k) for d in outer for k in range(2)]

    def inner_pairs():
        return [
            ((d, row_block(dx, dc) + k), 2 * row_at(d, dx, dc) + k)
            for d in inner
            for dx in range(nx)
            for dc in range(nc)
            for k in range(2)
        ]

    start_gather(0)
    for d in ls:
        col_forward(d)
    near_arrive(0)
    near_forward(0)
    col_done(0)
    upper(0)
    to_rows(0, outer)
    far_forward(0)
    to_rows(0, inner)
    near_done(0)
    split_plane(0, inner)
    quad = jnp.zeros((NRHS, TILE), F32)
    for at, block in inner_pairs():
        quad = quad + rowterm[(0, *at)] * rowbuf[0, block]
    for d in outer:
        plane_sum(0, d)
    for at, block in far_pairs():
        quad = quad + psum[(0, *at)] * rowbuf[0, block]
    quad = 2.0 * quad
    for k in range(2):
        quad = quad + masked_b[k] * diag_b[k]
    quad = coupling * quad
    for k in range(2):
        quad = quad + noise[k] * right[k] * right[k]
    red_send(0, 0, pack([right[0] * right[0] + right[1] * right[1], quad]))
    for d in inner:
        plane_sum(0, d)
    row_done(0)
    split_plane(0, outer)
    lower(0)
    red_send(0, 1, red_get(0, 0))
    total = row_final(0) + col_final(0)
    w = [
        noise[k] * right[k] + observed[k] * (coupling * (total[k] + diag_b[k]))
        for k in range(2)
    ]

    masked_w = [observed[k] * w[k] for k in range(2)]
    put_masked(1, masked_w)
    start_gather(1)
    diag_w = own_terms(masked_w)
    near_arrive(1)
    near_forward(1)
    col_done(1)
    upper(1)
    to_rows(1, outer)
    far_forward(1)
    to_rows(1, inner)
    near_done(1)
    split_plane(1, inner)
    first = red_get(0, 1)
    rr0, dad0 = unpack(first, 0), unpack(first, 1)
    alpha = rr0 / dad0
    res = [right[k] - alpha * w[k] for k in range(2)]
    red_send(
        1, 0, pack([res[0] * res[0] + res[1] * res[1], res[0] * w[0] + res[1] * w[1]])
    )
    quad = jnp.zeros((NRHS, TILE), F32)
    for at, block in inner_pairs():
        quad = quad + (rowterm[(0, *at)] - alpha * rowterm[(1, *at)]) * (
            rowbuf[0, block] - alpha * rowbuf[1, block]
        )
    for d in outer:
        plane_sum(1, d)
    for at, block in far_pairs():
        quad = quad + (psum[(0, *at)] - alpha * psum[(1, *at)]) * (
            rowbuf[0, block] - alpha * rowbuf[1, block]
        )
    quad = 2.0 * quad
    for k in range(2):
        quad = quad + (masked_b[k] - alpha * masked_w[k]) * (diag_b[k] - alpha * diag_w[k])
    quad = coupling * quad
    for k in range(2):
        quad = quad + noise[k] * res[k] * res[k]
    red_send(2, 0, pack([quad]))
    red_send(1, 1, red_get(1, 0))
    for d in inner:
        plane_sum(1, d)
    row_done(1)
    split_plane(1, outer)
    lower(1)
    red_send(2, 1, red_get(2, 0))
    total = row_final(1) + col_final(1)
    second = red_get(1, 1)
    rr1, rw1 = unpack(second, 0), unpack(second, 1)
    beta = rr1 / rr0
    u = [
        noise[k] * w[k] + observed[k] * (coupling * (total[k] + diag_w[k]))
        for k in range(2)
    ]
    third = unpack(red_get(2, 1), 0)
    dad1 = third + 2.0 * beta * rw1 + beta * beta * dad0
    alpha1 = rr1 / dad1
    for k in range(2):
        here = slice(k * TILE, (k + 1) * TILE)
        direction = res[k] + beta * right[k]
        image = (w[k] - alpha * u[k]) + beta * w[k]
        sol_ref[:, here] = alpha * right[k] + alpha1 * direction
        res_ref[:, here] = res[k] - alpha1 * image

    hops = 2 * (nzh - 1)
    sent(rowbuf.at[0, : 2 * hops], 0)
    sent(rowbuf.at[0, : 2 * len(ls)], 1)
    sent(rowbuf.at[0, : 2 * ((ny - 1) * nzl + ncol - 1)], 2)
    sent(rowbuf.at[:, : 2 * len(plane) * nzh], 3)
    sent(rowbuf.at[:, : 2 * len(plane) * nzh], 4)
    sent(rowbuf.at[0, : 4 * (ncol - 1)], 5)
    sent(rowbuf.at[0, : 2 * hops], 6)
    sent(red_dst, 7)


def local(
    rparts,
    cparts,
    right_sides,
    noise_var,
    observed,
    tile_data,
    diag_tiles,
    tile_rows,
    tile_cols,
    tile_count,
):
    slots = tile_data.shape[2]
    nzh, nx, nc = rparts
    ny, nzl = cparts
    nrow, ncol = nzh * nx * nc, ny * nzl
    plane = nx * nc - 1
    vmem = pl.BlockSpec(memory_space=pltpu.VMEM)
    hbm = pl.BlockSpec(memory_space=pltpu.HBM)
    dma = pltpu.SemaphoreType.DMA
    chunk = (2, NRHS, TILE)
    shape = jax.ShapeDtypeStruct(right_sides.shape, F32)
    return pl.pallas_call(
        functools.partial(kernel, rparts, cparts),
        out_shape=(shape, shape),
        in_specs=[hbm] * 8,
        out_specs=(vmem, vmem),
        scratch_shapes=[
            pltpu.VMEM(right_sides.shape, F32),
            pltpu.VMEM((1, 2 * TILE), F32),
            pltpu.VMEM((1, 2 * TILE), jnp.int32),
            pltpu.SMEM((slots,), jnp.int32),
            pltpu.SMEM((slots,), jnp.int32),
            pltpu.SMEM((1, 1), jnp.int32),
            pltpu.VMEM((slots, TILE, TILE), BF16),
            pltpu.VMEM((2, TILE, TILE), BF16),
            pltpu.VMEM((2, TILE, TILE), BF16),
            pltpu.VMEM((2 * nrow * NRHS, slots * NRHS), BF16),
            pltpu.VMEM((2 * ncol * NRHS, slots * NRHS), BF16),
            pltpu.VMEM((2, 2 * nrow, NRHS, TILE), F32),
            pltpu.VMEM((2, 2 * ncol, NRHS, TILE), F32),
            pltpu.VMEM((2 * nrow, 2 * NRHS, TILE), BF16),
            pltpu.VMEM((2 * ncol, 2 * NRHS, TILE), BF16),
            pltpu.VMEM((slots * NRHS, 2 * TILE), BF16),
            pltpu.VMEM((2, nzh, 2 * nx * nc, NRHS, TILE), F32),
            pltpu.VMEM((2, 2 * ncol, NRHS, TILE), F32),
            pltpu.VMEM((2, nzh, plane, *chunk), F32),
            pltpu.VMEM((2, nzh, *chunk), F32),
            pltpu.VMEM((2, nzh - 1, *chunk), F32),
            pltpu.VMEM((2, ncol - 1, *chunk), F32),
            pltpu.VMEM((3, 2, 1, TILE), F32),
            pltpu.VMEM((3, (plane + 1) * ny - 1 + nzh * nzl - 1, 1, TILE), F32),
            dma((8,)),
            dma((8,)),
            dma((2, 3)),
            dma((2, 2)),
            dma((nzl - 1,)),
            dma((2,)),
            dma((2, nzh)),
            dma((2,)),
            dma((2,)),
            dma((3, 2)),
        ],
        compiler_params=pltpu.CompilerParams(
            collective_id=0, has_side_effects=True, vmem_limit_bytes=67043328
        ),
        name="solve",
    )(
        right_sides,
        noise_var.reshape(1, -1),
        observed.reshape(1, -1),
        diag_tiles,
        tile_data.reshape(slots, TILE, TILE),
        tile_rows.reshape(slots),
        tile_cols.reshape(slots),
        tile_count,
    )


def solution(mesh):
    return jax.shard_map(
        functools.partial(local, ROW_PARTS, COL_PARTS),
        mesh=mesh,
        in_specs=(
            P(None, ("row", "col")),
            P(("row", "col")),
            P(("row", "col")),
            P("row", "col", None, None, None),
            P(("row", "col"), None, None),
            P("row", "col", None),
            P("row", "col", None),
            P("row", "col"),
        ),
        out_specs=(P(None, ("row", "col")), P(None, ("row", "col"))),
        check_vma=False,
    )
```

```python
import functools
import math

import jax
import jax.numpy as jnp
from jax import lax
from jax.experimental import pallas as pl
from jax.experimental.pallas import tpu as pltpu
from jax.sharding import PartitionSpec as P

TILE = 128
COUPLED = 32
NRHS = 8
MESH = pl.DeviceIdType.MESH
DIRECT = (True, False)
ROW_PARTS = (4, 4, 2)
COL_PARTS = (4, 4)
F32 = jnp.float32
BF16 = jnp.bfloat16


def split_rows(value):
    high = value.astype(BF16).astype(F32)
    return jnp.concatenate([high, value - high], axis=0).astype(BF16)


def near_first(size):
    return sorted(range(1, size), key=lambda d: min(d, size - d))


def kernel(
    rparts,
    cparts,
    rs_hbm,
    noise_hbm,
    obs_hbm,
    diag_hbm,
    tile_hbm,
    rows_hbm,
    cols_hbm,
    count_hbm,
    out_ref,
    rs_ref,
    noise_ref,
    obs_ref,
    rows_s,
    cols_s,
    count_s,
    tiles,
    diag,
    sym,
    hrow,
    hcol,
    rowbuf,
    colbuf,
    rowsplit,
    colsplit,
    both,
    rowterm,
    colterm,
    xrecv,
    psum,
    zrecv,
    yrecv,
    lsend,
    lrecv,
    red_src,
    red_dst,
    local_sem,
    sent_sem,
    agz_sem,
    agx_sem,
    agl_sem,
    agy_sem,
    rsx_sem,
    rsz_sem,
    rcy_sem,
    rcl_sem,
    red_sem,
):
    nzh, nx, nc = rparts
    ny, nzl = cparts
    nrow, ncol = nzh * nx * nc, ny * nzl
    slots = tile_hbm.shape[0]
    coupling = 1.0 / (2.0 * math.sqrt(TILE * (2 * COUPLED + 1)))

    row = lax.axis_index("row")
    col = lax.axis_index("col")
    zh, x, core = row // (nx * nc), row // nc % nx, row % nc
    y, zl = col // nzl, col % nzl

    def row_at(dz, dx, dc):
        return (
            lax.rem(zh + dz, nzh) * (nx * nc)
            + lax.rem(x + dx, nx) * nc
            + lax.rem(core + dc, nc)
        )

    def col_at(dy, dl):
        return lax.rem(y + dy, ny) * nzl + lax.rem(zl + dl, nzl)

    def row_from(dz, dx, dc):
        return row_at(nzh - dz, nx - dx, nc - dc)

    def col_from(dy, dl):
        return col_at(ny - dy, nzl - dl)

    plane = [(dx, dc) for dx in range(nx) for dc in range(nc) if dx or dc]
    plane = sorted(plane, key=lambda p: -min(p[0], nx - p[0]))
    line = [(dz, dl) for dz in range(nzh) for dl in range(nzl) if dz or dl]
    line = sorted(line, key=lambda p: -min(p[0] * nzl + p[1], nzh * nzl - p[0] * nzl - p[1]))
    ys, ls = near_first(ny), list(range(1, nzl))
    ring = [(dy, dl) for dy in range(ny) for dl in range(nzl) if dy or dl]
    ring = sorted(ring, key=lambda p: -min(p[0], ny - p[0]) - (2 if p[1] else 0))
    near = sorted({1, nzh - 1} - {0})
    far = 2 if nzh == 4 else None
    inner = [*near, 0]
    outer = [far] if far else []

    barrier = pltpu.get_barrier_semaphore()
    peers = [(row_at(d, 0, 0), col) for d in near]
    peers += [(row, col_at(0, d)) for d in ls]
    peers += [(row_at(0, dx, dc), col) for dx, dc in plane]
    peers += [(row, col_at(dy, 0)) for dy in ys]
    for peer in peers:
        pl.semaphore_signal(barrier, inc=1, device_id=peer, device_id_type=MESH)

    def remote(src, dst, kind, sem, device):
        return pltpu.make_async_remote_copy(
            src_ref=src,
            dst_ref=dst,
            send_sem=sent_sem.at[kind],
            recv_sem=sem,
            device_id=device,
            device_id_type=MESH,
        )

    def send(src, dst, kind, sem, device):
        remote(src, dst, kind, sem, device).start()

    def arrive(dst, sem):
        remote(dst, dst, 0, sem, (row, col)).wait_recv()

    def sent(src, kind):
        remote(src, src, kind, agz_sem.at[0, 0], (row, col)).wait_send()

    inputs = (
        (rs_hbm, rs_ref),
        (obs_hbm, obs_ref),
        (noise_hbm, noise_ref),
        (rows_hbm, rows_s),
        (cols_hbm, cols_s),
        (count_hbm, count_s),
        (diag_hbm, diag),
        (tile_hbm, tiles),
    )
    inputs = [
        pltpu.make_async_copy(src, dst, local_sem.at[k])
        for k, (src, dst) in enumerate(inputs)
    ]
    for copy in inputs:
        copy.start()
    for copy in inputs[:6]:
        copy.wait()

    observed = [obs_ref[:, k * TILE : (k + 1) * TILE].astype(F32) for k in range(2)]
    noise = [noise_ref[:, k * TILE : (k + 1) * TILE] for k in range(2)]
    right = [rs_ref[:, k * TILE : (k + 1) * TILE] for k in range(2)]

    def chunk_row(it, r):
        return rowbuf.at[it, pl.ds(2 * r, 2)]

    def chunk_col(it, c):
        return colbuf.at[it, pl.ds(2 * c, 2)]

    def put_masked(it, masked):
        for k in range(2):
            rowbuf[it, 2 * row + k] = masked[k]
            colbuf[it, 2 * col + k] = masked[k]

    def start_gather(it):
        mine_r, mine_c = chunk_row(it, row), chunk_col(it, col)
        for d in reversed(ls):
            send(mine_c, mine_c, 1, agl_sem.at[it, d - 1], (row, col_at(0, d)))
        if it and far:
            send(mine_r, mine_r, 0, agz_sem.at[it, 2], (row_at(far, 0, 0), col))
        for n, d in enumerate(near):
            send(mine_r, mine_r, 0, agz_sem.at[it, n], (row_at(d, 0, 0), col))
        for d in ys:
            send(mine_c, mine_c, 2, agy_sem.at[it], (row, col_at(d, 0)))
        for dx, dc in plane:
            send(mine_r, mine_r, 3, agx_sem.at[it, 0], (row_at(0, dx, dc), col))

    def col_forward(it, d):
        got = chunk_col(it, col_from(0, d))
        arrive(got, agl_sem.at[it, d - 1])
        for dy in ys:
            send(got, got, 2, agy_sem.at[it], (row, col_at(dy, 0)))

    def to_plane(it, got, late):
        for dx, dc in plane:
            send(got, got, 3, agx_sem.at[it, late], (row_at(0, dx, dc), col))

    def near_arrive(it):
        for n, d in enumerate(near):
            r = row_from(d, 0, 0)
            arrive(chunk_row(it, r), agz_sem.at[it, n])
            if far and not it:
                half = rowbuf.at[it, 2 * r + n]
                send(half, half, 0, agz_sem.at[it, 2], (row_at(d, 0, 0), col))

    def near_forward(it):
        for d in near:
            to_plane(it, chunk_row(it, row_from(d, 0, 0)), 0)

    def far_forward(it):
        if far:
            got = chunk_row(it, row_from(far, 0, 0))
            arrive(got, agz_sem.at[it, 2])
            to_plane(it, got, 1)

    def col_done(it):
        arrive(colbuf.at[it, : 2 * (ny - 1) * nzl], agy_sem.at[it])

    def near_done(it):
        arrive(rowbuf.at[it, : 2 * len(plane) * len(inner)], agx_sem.at[it, 0])

    def row_done(it):
        if far:
            arrive(rowbuf.at[it, : 2 * len(plane)], agx_sem.at[it, 1])

    def product(hot):
        sums = jnp.dot(hot, both[...], preferred_element_type=F32)
        return (sums[:, :TILE] + sums[:, TILE:]).reshape(hot.shape[0] // NRHS, NRHS, TILE)

    def terms(picks, pieces, contract):
        for t in range(0, slots, 2):
            left = jnp.concatenate([pieces[picks[t]], pieces[picks[t + 1]]], axis=0)
            if contract:
                pair = tiles[t : t + 2].reshape(2 * TILE, TILE)
            else:
                pair = jnp.concatenate([tiles[t], tiles[t + 1]], axis=1)
            sums = lax.dot_general(
                left, pair, (((1,), (contract,)), ((), ())), preferred_element_type=F32
            )
            value = []
            for k in range(2):
                part = sums[2 * NRHS * k : 2 * NRHS * (k + 1), TILE * k : TILE * (k + 1)]
                value.append(part[:NRHS] + part[NRHS:])
            value = jnp.concatenate(value, axis=0)
            high = value.astype(BF16)
            low = (value - high.astype(F32)).astype(BF16)
            both[t * NRHS : (t + 2) * NRHS] = jnp.concatenate([high, low], axis=1)

    def upper(it):
        for j in range(2 * ncol):
            colsplit[j] = split_rows(colbuf[it, j])
        terms(cols_s, colsplit, 1)

    def row_block(dx, dc):
        return 2 * (lax.rem(x + dx, nx) * nc + lax.rem(core + dc, nc))

    def to_rows(it, which):
        count = 2 * nx * nc * NRHS
        for dz in which:
            rowterm[it, dz] = product(hrow[dz * count : (dz + 1) * count])
        for dz in which:
            for p, (dx, dc) in enumerate(plane):
                send(
                    rowterm.at[it, dz, pl.ds(row_block(dx, dc), 2)],
                    xrecv.at[it, dz, p],
                    4,
                    rsx_sem.at[it, dz],
                    (row_at(0, dx, dc), col),
                )

    def split_chunk(it, r):
        for k in range(2):
            rowsplit[2 * r + k] = split_rows(rowbuf[it, 2 * r + k])

    def split_plane(it, which):
        for d in which:
            for dx in range(nx):
                for dc in range(nc):
                    split_chunk(it, row_at(d, dx, dc))

    def lower(it):
        terms(rows_s, rowsplit, 0)
        colterm[it] = product(hcol[...])
        if DIRECT[it]:
            for n, (dy, dl) in enumerate(ring):
                send(
                    colterm.at[it, pl.ds(2 * col_at(dy, dl), 2)],
                    yrecv.at[it, n],
                    5,
                    rcy_sem.at[it, 0],
                    (row, col_at(dy, dl)),
                )
            return
        for dl in [*ls, 0]:
            for n, dy in enumerate(ys):
                send(
                    colterm.at[it, pl.ds(2 * col_at(dy, dl), 2)],
                    yrecv.at[it, dl * len(ys) + n],
                    5,
                    rcy_sem.at[it, 1 if dl else 2],
                    (row, col_at(dy, 0)),
                )

    def col_reduce(it):
        if DIRECT[it]:
            return
        count = len(ys)
        arrive(yrecv.at[it, count : count * nzl], rcy_sem.at[it, 1])
        for dl in ls:
            total = colterm[it, pl.ds(2 * col_at(0, dl), 2)]
            for n in range(count):
                total = total + yrecv[it, dl * count + n]
            lsend[it, dl - 1] = total
            send(
                lsend.at[it, dl - 1], lrecv.at[it, dl - 1], 6, rcl_sem.at[it], (row, col_at(0, dl))
            )

    def plane_sum(it, dz):
        arrive(xrecv.at[it, dz], rsx_sem.at[it, dz])
        total = rowterm[it, dz, pl.ds(row_block(0, 0), 2)]
        for p in range(len(plane)):
            total = total + xrecv[it, dz, p]
        psum[it, dz] = total
        if dz:
            send(psum.at[it, dz], zrecv.at[it, dz - 1], 6, rsz_sem.at[it], (row_at(dz, 0, 0), col))

    def row_final(it):
        total = psum[it, 0]
        arrive(zrecv.at[it], rsz_sem.at[it])
        for d in range(nzh - 1):
            total = total + zrecv[it, d]
        return total

    def col_final(it):
        total = colterm[it, pl.ds(2 * col, 2)]
        if DIRECT[it]:
            arrive(yrecv.at[it], rcy_sem.at[it, 0])
            for n in range(ncol - 1):
                total = total + yrecv[it, n]
            return total
        arrive(yrecv.at[it, : len(ys)], rcy_sem.at[it, 2])
        for n in range(len(ys)):
            total = total + yrecv[it, n]
        arrive(lrecv.at[it], rcl_sem.at[it])
        for n in range(nzl - 1):
            total = total + lrecv[it, n]
        return total

    lane = lax.broadcasted_iota(jnp.int32, (NRHS, TILE), 1)
    sub = lax.broadcasted_iota(jnp.int32, (NRHS, TILE), 0)
    slab = [(dx, dc, dy) for dx, dc in [*plane, (0, 0)] for dy in [*reversed(ys), 0]]
    stages = (
        [(row_at(0, dx, dc), col_at(dy, 0)) for dx, dc, dy in slab[:-1]],
        [(row_at(dz, 0, 0), col_at(0, dl)) for dz, dl in line],
    )
    first_slot = (0, len(slab) - 1)

    def red_send(r, stage, value):
        red_src[r, stage] = value
        for n, device in enumerate(stages[stage]):
            send(
                red_src.at[r, stage],
                red_dst.at[r, first_slot[stage] + n],
                7,
                red_sem.at[r, stage],
                device,
            )

    def red_get(r, stage):
        count = len(stages[stage])
        arrive(red_dst.at[r, pl.ds(first_slot[stage], count)], red_sem.at[r, stage])
        total = red_src[r, stage]
        for n in range(count):
            total = total + red_dst[r, first_slot[stage] + n]
        return total

    def pack(values):
        packed = jnp.zeros((NRHS, TILE), F32)
        for k, value in enumerate(values):
            whole = jnp.sum(value, axis=1, keepdims=True)
            packed = packed + jnp.where(lane == sub + NRHS * k, whole, 0.0)
        return jnp.sum(packed, axis=0, keepdims=True)

    def unpack(total, k):
        return jnp.sum(jnp.where(lane == sub + NRHS * k, total, 0.0), axis=1, keepdims=True)

    masked_b = [observed[k] * right[k] for k in range(2)]
    put_masked(0, masked_b)

    def hot_matrices():
        wide = lax.broadcasted_iota(jnp.int32, (1, slots * NRHS), 1)
        row_index = jnp.zeros((1, slots * NRHS), jnp.int32)
        col_index = jnp.zeros((1, slots * NRHS), jnp.int32)
        for t in range(slots):
            here = wide // NRHS == t
            row_index = jnp.where(here, rows_s[t] * NRHS, row_index)
            col_index = jnp.where(here, cols_s[t] * NRHS, col_index)
        here = 2 * nx * nc * NRHS
        row_index = (row_index // here + (nzh - zh)) % nzh * here + row_index % here
        live = wide // NRHS < count_s[0, 0]
        row_index = jnp.where(live, row_index + wide % NRHS, -1)
        col_index = jnp.where(live, col_index + wide % NRHS, -1)
        step = 64
        for ref, index in ((hrow, row_index), (hcol, col_index)):
            for start in range(0, ref.shape[0], step):
                at = lax.broadcasted_iota(jnp.int32, (step, slots * NRHS), 0) + start
                ref[start : start + step] = jnp.where(at == index, 1.0, 0.0).astype(BF16)

    def own_terms(masked):
        out = []
        for k in range(2):
            both = jnp.dot(split_rows(masked[k]), sym[k], preferred_element_type=F32)
            out.append(both[:NRHS] + both[NRHS:])
        return out

    hot_matrices()
    inputs[6].wait()
    a_index = lax.broadcasted_iota(jnp.int32, (TILE, TILE), 0)
    b_index = lax.broadcasted_iota(jnp.int32, (TILE, TILE), 1)
    for k in range(2):
        block = diag[k].astype(F32)
        sym[k] = jnp.where(b_index >= a_index, block, block.T).astype(BF16)
    diag_b = own_terms(masked_b)
    inputs[7].wait()

    pl.semaphore_wait(barrier, len(peers))

    def far_pairs():
        return [((d, k), 2 * row_at(d, 0, 0) + k) for d in outer for k in range(2)]

    def inner_pairs():
        return [
            ((d, row_block(dx, dc) + k), 2 * row_at(d, dx, dc) + k)
            for d in inner
            for dx in range(nx)
            for dc in range(nc)
            for k in range(2)
        ]

    start_gather(0)
    for d in ls:
        col_forward(0, d)
    near_arrive(0)
    near_forward(0)
    col_done(0)
    upper(0)
    to_rows(0, outer)
    to_rows(0, inner)
    far_forward(0)
    near_done(0)
    split_plane(0, inner)
    quad = jnp.zeros((NRHS, TILE), F32)
    for at, block in inner_pairs():
        quad = quad + rowterm[(0, *at)] * rowbuf[0, block]
    for d in outer:
        plane_sum(0, d)
    for at, block in far_pairs():
        quad = quad + psum[(0, *at)] * rowbuf[0, block]
    quad = 2.0 * quad
    for k in range(2):
        quad = quad + masked_b[k] * diag_b[k]
    quad = coupling * quad
    for k in range(2):
        quad = quad + noise[k] * right[k] * right[k]
    red_send(0, 0, pack([right[0] * right[0] + right[1] * right[1], quad]))
    for d in inner:
        plane_sum(0, d)
    row_done(0)
    split_plane(0, outer)
    lower(0)
    col_reduce(0)
    red_send(0, 1, red_get(0, 0))
    total = row_final(0) + col_final(0)
    w = [
        noise[k] * right[k] + observed[k] * (coupling * (total[k] + diag_b[k]))
        for k in range(2)
    ]

    masked_w = [observed[k] * w[k] for k in range(2)]
    put_masked(1, masked_w)
    start_gather(1)
    diag_w = own_terms(masked_w)
    for d in ls:
        col_forward(1, d)
    near_arrive(1)
    near_forward(1)
    col_done(1)
    upper(1)
    to_rows(1, outer)
    to_rows(1, inner)
    far_forward(1)
    near_done(1)
    split_plane(1, inner)
    first = red_get(0, 1)
    rr0, dad0 = unpack(first, 0), unpack(first, 1)
    alpha = rr0 / dad0
    res = [right[k] - alpha * w[k] for k in range(2)]
    red_send(
        1, 0, pack([res[0] * res[0] + res[1] * res[1], res[0] * w[0] + res[1] * w[1]])
    )
    quad = jnp.zeros((NRHS, TILE), F32)
    for at, block in inner_pairs():
        quad = quad + (rowterm[(0, *at)] - alpha * rowterm[(1, *at)]) * (
            rowbuf[0, block] - alpha * rowbuf[1, block]
        )
    for d in outer:
        plane_sum(1, d)
    for at, block in far_pairs():
        quad = quad + (psum[(0, *at)] - alpha * psum[(1, *at)]) * (
            rowbuf[0, block] - alpha * rowbuf[1, block]
        )
    quad = 2.0 * quad
    for k in range(2):
        quad = quad + (masked_b[k] - alpha * masked_w[k]) * (diag_b[k] - alpha * diag_w[k])
    quad = coupling * quad
    for k in range(2):
        quad = quad + noise[k] * res[k] * res[k]
    red_send(2, 0, pack([quad]))
    red_send(1, 1, red_get(1, 0))
    for d in inner:
        plane_sum(1, d)
    row_done(1)
    split_plane(1, outer)
    lower(1)
    red_send(2, 1, red_get(2, 0))
    col_reduce(1)
    total = row_final(1) + col_final(1)
    second = red_get(1, 1)
    rr1, rw1 = unpack(second, 0), unpack(second, 1)
    beta = rr1 / rr0
    u = [
        noise[k] * w[k] + observed[k] * (coupling * (total[k] + diag_w[k]))
        for k in range(2)
    ]
    third = unpack(red_get(2, 1), 0)
    dad1 = third + 2.0 * beta * rw1 + beta * beta * dad0
    alpha1 = rr1 / dad1
    for k in range(2):
        here = slice(k * TILE, (k + 1) * TILE)
        direction = res[k] + beta * right[k]
        image = (w[k] - alpha * u[k]) + beta * w[k]
        out_ref[0, :, here] = alpha * right[k] + alpha1 * direction
        out_ref[1, :, here] = res[k] - alpha1 * image

    hops = 2 * (nzh - 1)
    sent(rowbuf.at[0, : 2 * hops], 0)
    sent(rowbuf.at[0, : 4 * len(ls)], 1)
    sent(rowbuf.at[:, : 2 * (ny - 1) * nzl], 2)
    sent(rowbuf.at[:, : 2 * len(plane) * nzh], 3)
    sent(rowbuf.at[:, : 2 * len(plane) * nzh], 4)
    counts = [ncol - 1 if DIRECT[it] else (ny - 1) * nzl for it in range(2)]
    sent(rowbuf.at[0, : 2 * sum(counts)], 5)
    extra = sum(0 if DIRECT[it] else nzl - 1 for it in range(2))
    sent(rowbuf.at[0, : 2 * (hops + extra)], 6)
    sent(red_dst, 7)


def local(
    rparts,
    cparts,
    right_sides,
    noise_var,
    observed,
    tile_data,
    diag_tiles,
    tile_rows,
    tile_cols,
    tile_count,
):
    slots = tile_data.shape[2]
    nzh, nx, nc = rparts
    ny, nzl = cparts
    nrow, ncol = nzh * nx * nc, ny * nzl
    plane = nx * nc - 1
    vmem = pl.BlockSpec(memory_space=pltpu.VMEM)
    hbm = pl.BlockSpec(memory_space=pltpu.HBM)
    dma = pltpu.SemaphoreType.DMA
    chunk = (2, NRHS, TILE)
    shape = jax.ShapeDtypeStruct((2, *right_sides.shape), F32)
    out = pl.pallas_call(
        functools.partial(kernel, rparts, cparts),
        out_shape=shape,
        in_specs=[hbm] * 8,
        out_specs=vmem,
        scratch_shapes=[
            pltpu.VMEM(right_sides.shape, F32),
            pltpu.VMEM((1, 2 * TILE), F32),
            pltpu.VMEM((1, 2 * TILE), jnp.int32),
            pltpu.SMEM((slots,), jnp.int32),
            pltpu.SMEM((slots,), jnp.int32),
            pltpu.SMEM((1, 1), jnp.int32),
            pltpu.VMEM((slots, TILE, TILE), BF16),
            pltpu.VMEM((2, TILE, TILE), BF16),
            pltpu.VMEM((2, TILE, TILE), BF16),
            pltpu.VMEM((2 * nrow * NRHS, slots * NRHS), BF16),
            pltpu.VMEM((2 * ncol * NRHS, slots * NRHS), BF16),
            pltpu.VMEM((2, 2 * nrow, NRHS, TILE), F32),
            pltpu.VMEM((2, 2 * ncol, NRHS, TILE), F32),
            pltpu.VMEM((2 * nrow, 2 * NRHS, TILE), BF16),
            pltpu.VMEM((2 * ncol, 2 * NRHS, TILE), BF16),
            pltpu.VMEM((slots * NRHS, 2 * TILE), BF16),
            pltpu.VMEM((2, nzh, 2 * nx * nc, NRHS, TILE), F32),
            pltpu.VMEM((2, 2 * ncol, NRHS, TILE), F32),
            pltpu.VMEM((2, nzh, plane, *chunk), F32),
            pltpu.VMEM((2, nzh, *chunk), F32),
            pltpu.VMEM((2, nzh - 1, *chunk), F32),
            pltpu.VMEM((2, ncol - 1, *chunk), F32),
            pltpu.VMEM((2, nzl - 1, *chunk), F32),
            pltpu.VMEM((2, nzl - 1, *chunk), F32),
            pltpu.VMEM((3, 2, 1, TILE), F32),
            pltpu.VMEM((3, (plane + 1) * ny - 1 + nzh * nzl - 1, 1, TILE), F32),
            dma((8,)),
            dma((8,)),
            dma((2, 3)),
            dma((2, 2)),
            dma((2, nzl - 1)),
            dma((2,)),
            dma((2, nzh)),
            dma((2,)),
            dma((2, 3)),
            dma((2,)),
            dma((3, 2)),
        ],
        compiler_params=pltpu.CompilerParams(
            collective_id=0, has_side_effects=True, vmem_limit_bytes=67043328
        ),
        name="solve",
    )(
        right_sides,
        noise_var.reshape(1, -1),
        observed.reshape(1, -1),
        diag_tiles,
        tile_data.reshape(slots, TILE, TILE),
        tile_rows.reshape(slots),
        tile_cols.reshape(slots),
        tile_count,
    )
    return out[0], out[1]


def solution(mesh):
    return jax.shard_map(
        functools.partial(local, ROW_PARTS, COL_PARTS),
        mesh=mesh,
        in_specs=(
            P(None, ("row", "col")),
            P(("row", "col")),
            P(("row", "col")),
            P("row", "col", None, None, None),
            P(("row", "col"), None, None),
            P("row", "col", None),
            P("row", "col", None),
            P("row", "col"),
        ),
        out_specs=(P(None, ("row", "col")), P(None, ("row", "col"))),
        check_vma=False,
    )
```

```python
import functools
import math

import jax
import jax.numpy as jnp
from jax import lax
from jax.experimental import pallas as pl
from jax.experimental.pallas import tpu as pltpu
from jax.sharding import PartitionSpec as P

TILE = 128
COUPLED = 32
NRHS = 8
MESH = pl.DeviceIdType.MESH
DIRECT = (True, False)
ROW_PARTS = (4, 4, 2)
COL_PARTS = (4, 4)
F32 = jnp.float32
BF16 = jnp.bfloat16


def split_rows(value):
    high = value.astype(BF16).astype(F32)
    return jnp.concatenate([high, value - high], axis=0).astype(BF16)


def near_first(size):
    return sorted(range(1, size), key=lambda d: min(d, size - d))


def kernel(
    rparts,
    cparts,
    rs_hbm,
    noise_hbm,
    obs_hbm,
    diag_hbm,
    tile_hbm,
    rows_hbm,
    cols_hbm,
    count_hbm,
    out_ref,
    rs_ref,
    noise_ref,
    obs_ref,
    rows_s,
    cols_s,
    count_s,
    tiles,
    diag,
    sym,
    hrow,
    hcol,
    rowbuf,
    colbuf,
    rowsplit,
    colsplit,
    both,
    rowterm,
    colterm,
    xrecv,
    psum,
    zrecv,
    yrecv,
    lsend,
    lrecv,
    red_src,
    red_dst,
    local_sem,
    sent_sem,
    agz_sem,
    agx_sem,
    agl_sem,
    agy_sem,
    rsx_sem,
    rsz_sem,
    rcy_sem,
    rcl_sem,
    red_sem,
):
    nzh, nx, nc = rparts
    ny, nzl = cparts
    nrow, ncol = nzh * nx * nc, ny * nzl
    slots = tile_hbm.shape[0]
    coupling = 1.0 / (2.0 * math.sqrt(TILE * (2 * COUPLED + 1)))

    row = lax.axis_index("row")
    col = lax.axis_index("col")
    zh, x, core = row // (nx * nc), row // nc % nx, row % nc
    y, zl = col // nzl, col % nzl

    def row_at(dz, dx, dc):
        return (
            lax.rem(zh + dz, nzh) * (nx * nc)
            + lax.rem(x + dx, nx) * nc
            + lax.rem(core + dc, nc)
        )

    def col_at(dy, dl):
        return lax.rem(y + dy, ny) * nzl + lax.rem(zl + dl, nzl)

    def row_from(dz, dx, dc):
        return row_at(nzh - dz, nx - dx, nc - dc)

    def col_from(dy, dl):
        return col_at(ny - dy, nzl - dl)

    plane = [(dx, dc) for dx in range(nx) for dc in range(nc) if dx or dc]
    plane = sorted(plane, key=lambda p: -min(p[0], nx - p[0]))
    line = [(dz, dl) for dz in range(nzh) for dl in range(nzl) if dz or dl]
    line = sorted(line, key=lambda p: -min(p[0] * nzl + p[1], nzh * nzl - p[0] * nzl - p[1]))
    ys, ls = near_first(ny), list(range(1, nzl))
    ring = [(dy, dl) for dy in range(ny) for dl in range(nzl) if dy or dl]
    ring = sorted(ring, key=lambda p: -min(p[0], ny - p[0]) - (2 if p[1] else 0))
    near = sorted({1, nzh - 1} - {0})
    far = 2 if nzh == 4 else None
    inner = [*near, 0]
    outer = [far] if far else []

    barrier = pltpu.get_barrier_semaphore()
    peers = [(row_at(d, 0, 0), col) for d in near]
    peers += [(row, col_at(0, d)) for d in ls]
    peers += [(row_at(0, dx, dc), col) for dx, dc in plane]
    peers += [(row, col_at(dy, 0)) for dy in ys]
    for peer in peers:
        pl.semaphore_signal(barrier, inc=1, device_id=peer, device_id_type=MESH)

    def remote(src, dst, kind, sem, device):
        return pltpu.make_async_remote_copy(
            src_ref=src,
            dst_ref=dst,
            send_sem=sent_sem.at[kind],
            recv_sem=sem,
            device_id=device,
            device_id_type=MESH,
        )

    def send(src, dst, kind, sem, device):
        remote(src, dst, kind, sem, device).start()

    def arrive(dst, sem):
        remote(dst, dst, 0, sem, (row, col)).wait_recv()

    def sent(src, kind):
        remote(src, src, kind, agz_sem.at[0, 0], (row, col)).wait_send()

    inputs = (
        (rs_hbm, rs_ref),
        (obs_hbm, obs_ref),
        (noise_hbm, noise_ref),
        (rows_hbm, rows_s),
        (cols_hbm, cols_s),
        (count_hbm, count_s),
        (diag_hbm, diag),
        (tile_hbm, tiles),
    )
    inputs = [
        pltpu.make_async_copy(src, dst, local_sem.at[k])
        for k, (src, dst) in enumerate(inputs)
    ]
    for copy in inputs:
        copy.start()
    for copy in inputs[:6]:
        copy.wait()

    observed = [obs_ref[:, k * TILE : (k + 1) * TILE].astype(F32) for k in range(2)]
    noise = [noise_ref[:, k * TILE : (k + 1) * TILE] for k in range(2)]
    right = [rs_ref[:, k * TILE : (k + 1) * TILE] for k in range(2)]

    def chunk_row(it, r):
        return rowbuf.at[it, pl.ds(2 * r, 2)]

    def chunk_col(it, c):
        return colbuf.at[it, pl.ds(2 * c, 2)]

    def put_masked(it, masked):
        for k in range(2):
            rowbuf[it, 2 * row + k] = masked[k]
            colbuf[it, 2 * col + k] = masked[k]

    def start_gather(it):
        mine_r, mine_c = chunk_row(it, row), chunk_col(it, col)
        for d in reversed(ls):
            send(mine_c, mine_c, 1, agl_sem.at[it, d - 1], (row, col_at(0, d)))
        if it and far:
            send(mine_r, mine_r, 0, agz_sem.at[it, 2], (row_at(far, 0, 0), col))
        for n, d in enumerate(near):
            send(mine_r, mine_r, 0, agz_sem.at[it, n], (row_at(d, 0, 0), col))
        for d in ys:
            send(mine_c, mine_c, 2, agy_sem.at[it], (row, col_at(d, 0)))
        for dx, dc in plane:
            send(mine_r, mine_r, 3, agx_sem.at[it, 0], (row_at(0, dx, dc), col))

    def col_forward(it, d):
        got = chunk_col(it, col_from(0, d))
        arrive(got, agl_sem.at[it, d - 1])
        for dy in ys:
            send(got, got, 2, agy_sem.at[it], (row, col_at(dy, 0)))

    def to_plane(it, got, late):
        for dx, dc in plane:
            send(got, got, 3, agx_sem.at[it, late], (row_at(0, dx, dc), col))

    def near_arrive(it):
        for n, d in enumerate(near):
            r = row_from(d, 0, 0)
            arrive(chunk_row(it, r), agz_sem.at[it, n])
            if far and not it:
                half = rowbuf.at[it, 2 * r + n]
                send(half, half, 0, agz_sem.at[it, 2], (row_at(d, 0, 0), col))

    def near_forward(it):
        for d in near:
            to_plane(it, chunk_row(it, row_from(d, 0, 0)), 0)

    def far_forward(it):
        if far:
            got = chunk_row(it, row_from(far, 0, 0))
            arrive(got, agz_sem.at[it, 2])
            to_plane(it, got, 1)

    def col_done(it):
        arrive(colbuf.at[it, : 2 * (ny - 1) * nzl], agy_sem.at[it])

    def near_done(it):
        arrive(rowbuf.at[it, : 2 * len(plane) * len(inner)], agx_sem.at[it, 0])

    def row_done(it):
        if far:
            arrive(rowbuf.at[it, : 2 * len(plane)], agx_sem.at[it, 1])

    def product(hot):
        sums = jnp.dot(hot, both[...], preferred_element_type=F32)
        return (sums[:, :TILE] + sums[:, TILE:]).reshape(hot.shape[0] // NRHS, NRHS, TILE)

    def terms(picks, pieces, contract):
        for t in range(0, slots, 2):
            left = jnp.concatenate([pieces[picks[t]], pieces[picks[t + 1]]], axis=0)
            if contract:
                pair = tiles[t : t + 2].reshape(2 * TILE, TILE)
            else:
                pair = jnp.concatenate([tiles[t], tiles[t + 1]], axis=1)
            sums = lax.dot_general(
                left, pair, (((1,), (contract,)), ((), ())), preferred_element_type=F32
            )
            value = []
            for k in range(2):
                part = sums[2 * NRHS * k : 2 * NRHS * (k + 1), TILE * k : TILE * (k + 1)]
                value.append(part[:NRHS] + part[NRHS:])
            value = jnp.concatenate(value, axis=0)
            high = value.astype(BF16)
            low = (value - high.astype(F32)).astype(BF16)
            both[t * NRHS : (t + 2) * NRHS] = jnp.concatenate([high, low], axis=1)

    def upper(it):
        for j in range(2 * ncol):
            colsplit[j] = split_rows(colbuf[it, j])
        terms(cols_s, colsplit, 1)

    def row_block(dx, dc):
        return 2 * (lax.rem(x + dx, nx) * nc + lax.rem(core + dc, nc))

    def to_rows(it, which):
        count = 2 * nx * nc * NRHS
        for dz in which:
            rowterm[it, dz] = product(hrow[dz * count : (dz + 1) * count])
        for dz in which:
            for p, (dx, dc) in enumerate(plane):
                send(
                    rowterm.at[it, dz, pl.ds(row_block(dx, dc), 2)],
                    xrecv.at[it, dz, p],
                    4,
                    rsx_sem.at[it, dz],
                    (row_at(0, dx, dc), col),
                )

    def split_chunk(it, r):
        for k in range(2):
            rowsplit[2 * r + k] = split_rows(rowbuf[it, 2 * r + k])

    def split_plane(it, which):
        for d in which:
            for dx in range(nx):
                for dc in range(nc):
                    split_chunk(it, row_at(d, dx, dc))

    def lower(it):
        terms(rows_s, rowsplit, 0)
        colterm[it] = product(hcol[...])
        if DIRECT[it]:
            for n, (dy, dl) in enumerate(ring):
                send(
                    colterm.at[it, pl.ds(2 * col_at(dy, dl), 2)],
                    yrecv.at[it, n],
                    5,
                    rcy_sem.at[it, 0],
                    (row, col_at(dy, dl)),
                )
            return
        for dl in [*ls, 0]:
            for n, dy in enumerate(ys):
                send(
                    colterm.at[it, pl.ds(2 * col_at(dy, dl), 2)],
                    yrecv.at[it, dl * len(ys) + n],
                    5,
                    rcy_sem.at[it, 1 if dl else 2],
                    (row, col_at(dy, 0)),
                )

    def col_reduce(it):
        if DIRECT[it]:
            return
        count = len(ys)
        arrive(yrecv.at[it, count : count * nzl], rcy_sem.at[it, 1])
        for dl in ls:
            total = colterm[it, pl.ds(2 * col_at(0, dl), 2)]
            for n in range(count):
                total = total + yrecv[it, dl * count + n]
            lsend[it, dl - 1] = total
            send(
                lsend.at[it, dl - 1], lrecv.at[it, dl - 1], 6, rcl_sem.at[it], (row, col_at(0, dl))
            )

    def plane_sum(it, dz):
        arrive(xrecv.at[it, dz], rsx_sem.at[it, dz])
        total = rowterm[it, dz, pl.ds(row_block(0, 0), 2)]
        for p in range(len(plane)):
            total = total + xrecv[it, dz, p]
        psum[it, dz] = total
        if dz:
            send(psum.at[it, dz], zrecv.at[it, dz - 1], 6, rsz_sem.at[it], (row_at(dz, 0, 0), col))

    def row_final(it):
        total = psum[it, 0]
        arrive(zrecv.at[it], rsz_sem.at[it])
        for d in range(nzh - 1):
            total = total + zrecv[it, d]
        return total

    def col_final(it):
        total = colterm[it, pl.ds(2 * col, 2)]
        if DIRECT[it]:
            arrive(yrecv.at[it], rcy_sem.at[it, 0])
            for n in range(ncol - 1):
                total = total + yrecv[it, n]
            return total
        arrive(yrecv.at[it, : len(ys)], rcy_sem.at[it, 2])
        for n in range(len(ys)):
            total = total + yrecv[it, n]
        arrive(lrecv.at[it], rcl_sem.at[it])
        for n in range(nzl - 1):
            total = total + lrecv[it, n]
        return total

    lane = lax.broadcasted_iota(jnp.int32, (NRHS, TILE), 1)
    sub = lax.broadcasted_iota(jnp.int32, (NRHS, TILE), 0)
    slab = [(dx, dc, dy) for dx, dc in [*plane, (0, 0)] for dy in [*reversed(ys), 0]]
    stages = (
        [(row_at(0, dx, dc), col_at(dy, 0)) for dx, dc, dy in slab[:-1]],
        [(row_at(dz, 0, 0), col_at(0, dl)) for dz, dl in line],
    )
    first_slot = (0, len(slab) - 1)

    def red_send(r, stage, value):
        red_src[r, stage] = value
        for n, device in enumerate(stages[stage]):
            send(
                red_src.at[r, stage],
                red_dst.at[r, first_slot[stage] + n],
                7,
                red_sem.at[r, stage],
                device,
            )

    def red_get(r, stage):
        count = len(stages[stage])
        arrive(red_dst.at[r, pl.ds(first_slot[stage], count)], red_sem.at[r, stage])
        total = red_src[r, stage]
        for n in range(count):
            total = total + red_dst[r, first_slot[stage] + n]
        return total

    def pack(values):
        packed = jnp.zeros((NRHS, TILE), F32)
        for k, value in enumerate(values):
            whole = jnp.sum(value, axis=1, keepdims=True)
            packed = packed + jnp.where(lane == sub + NRHS * k, whole, 0.0)
        return jnp.sum(packed, axis=0, keepdims=True)

    def unpack(total, k):
        return jnp.sum(jnp.where(lane == sub + NRHS * k, total, 0.0), axis=1, keepdims=True)

    masked_b = [observed[k] * right[k] for k in range(2)]
    put_masked(0, masked_b)

    def hot_matrices():
        wide = lax.broadcasted_iota(jnp.int32, (1, slots * NRHS), 1)
        row_index = jnp.zeros((1, slots * NRHS), jnp.int32)
        col_index = jnp.zeros((1, slots * NRHS), jnp.int32)
        for t in range(slots):
            here = wide // NRHS == t
            row_index = jnp.where(here, rows_s[t] * NRHS, row_index)
            col_index = jnp.where(here, cols_s[t] * NRHS, col_index)
        here = 2 * nx * nc * NRHS
        row_index = (row_index // here + (nzh - zh)) % nzh * here + row_index % here
        live = wide // NRHS < count_s[0, 0]
        row_index = jnp.where(live, row_index + wide % NRHS, -1)
        col_index = jnp.where(live, col_index + wide % NRHS, -1)
        step = 64
        for ref, index in ((hrow, row_index), (hcol, col_index)):
            for start in range(0, ref.shape[0], step):
                at = lax.broadcasted_iota(jnp.int32, (step, slots * NRHS), 0) + start
                ref[start : start + step] = jnp.where(at == index, 1.0, 0.0).astype(BF16)

    def own_terms(masked):
        out = []
        for k in range(2):
            both = jnp.dot(split_rows(masked[k]), sym[k], preferred_element_type=F32)
            out.append(both[:NRHS] + both[NRHS:])
        return out

    hot_matrices()
    inputs[6].wait()
    a_index = lax.broadcasted_iota(jnp.int32, (TILE, TILE), 0)
    b_index = lax.broadcasted_iota(jnp.int32, (TILE, TILE), 1)
    for k in range(2):
        block = diag[k].astype(F32)
        sym[k] = jnp.where(b_index >= a_index, block, block.T).astype(BF16)
    diag_b = own_terms(masked_b)
    inputs[7].wait()

    pl.semaphore_wait(barrier, len(peers))

    def far_pairs():
        return [((d, k), 2 * row_at(d, 0, 0) + k) for d in outer for k in range(2)]

    def inner_pairs():
        return [
            ((d, row_block(dx, dc) + k), 2 * row_at(d, dx, dc) + k)
            for d in inner
            for dx in range(nx)
            for dc in range(nc)
            for k in range(2)
        ]

    start_gather(0)
    for d in ls:
        col_forward(0, d)
    near_arrive(0)
    near_forward(0)
    col_done(0)
    upper(0)
    to_rows(0, outer)
    to_rows(0, inner)
    far_forward(0)
    near_done(0)
    split_plane(0, inner)
    quad = jnp.zeros((NRHS, TILE), F32)
    for at, block in inner_pairs():
        quad = quad + rowterm[(0, *at)] * rowbuf[0, block]
    for d in outer:
        plane_sum(0, d)
    for at, block in far_pairs():
        quad = quad + psum[(0, *at)] * rowbuf[0, block]
    quad = 2.0 * quad
    for k in range(2):
        quad = quad + masked_b[k] * diag_b[k]
    quad = coupling * quad
    for k in range(2):
        quad = quad + noise[k] * right[k] * right[k]
    red_send(0, 0, pack([right[0] * right[0] + right[1] * right[1], quad]))
    for d in inner:
        plane_sum(0, d)
    row_done(0)
    split_plane(0, outer)
    lower(0)
    col_reduce(0)
    red_send(0, 1, red_get(0, 0))
    total = row_final(0) + col_final(0)
    w = [
        noise[k] * right[k] + observed[k] * (coupling * (total[k] + diag_b[k]))
        for k in range(2)
    ]

    masked_w = [observed[k] * w[k] for k in range(2)]
    put_masked(1, masked_w)
    start_gather(1)
    diag_w = own_terms(masked_w)
    for d in ls:
        col_forward(1, d)
    near_arrive(1)
    near_forward(1)
    col_done(1)
    upper(1)
    to_rows(1, outer)
    to_rows(1, inner)
    far_forward(1)
    first = red_get(0, 1)
    rr0, dad0 = unpack(first, 0), unpack(first, 1)
    alpha = rr0 / dad0
    res = [right[k] - alpha * w[k] for k in range(2)]
    red_send(
        1, 0, pack([res[0] * res[0] + res[1] * res[1], res[0] * w[0] + res[1] * w[1]])
    )
    near_done(1)
    split_plane(1, inner)
    quad = jnp.zeros((NRHS, TILE), F32)
    for at, block in inner_pairs():
        quad = quad + (rowterm[(0, *at)] - alpha * rowterm[(1, *at)]) * (
            rowbuf[0, block] - alpha * rowbuf[1, block]
        )
    for d in outer:
        plane_sum(1, d)
    for at, block in far_pairs():
        quad = quad + (psum[(0, *at)] - alpha * psum[(1, *at)]) * (
            rowbuf[0, block] - alpha * rowbuf[1, block]
        )
    quad = 2.0 * quad
    for k in range(2):
        quad = quad + (masked_b[k] - alpha * masked_w[k]) * (diag_b[k] - alpha * diag_w[k])
    quad = coupling * quad
    for k in range(2):
        quad = quad + noise[k] * res[k] * res[k]
    red_send(2, 0, pack([quad]))
    for d in inner:
        plane_sum(1, d)
    row_done(1)
    split_plane(1, outer)
    lower(1)
    red_send(1, 1, red_get(1, 0))
    red_send(2, 1, red_get(2, 0))
    col_reduce(1)
    total = row_final(1) + col_final(1)
    second = red_get(1, 1)
    rr1, rw1 = unpack(second, 0), unpack(second, 1)
    beta = rr1 / rr0
    u = [
        noise[k] * w[k] + observed[k] * (coupling * (total[k] + diag_w[k]))
        for k in range(2)
    ]
    third = unpack(red_get(2, 1), 0)
    dad1 = third + 2.0 * beta * rw1 + beta * beta * dad0
    alpha1 = rr1 / dad1
    for k in range(2):
        here = slice(k * TILE, (k + 1) * TILE)
        direction = res[k] + beta * right[k]
        image = (w[k] - alpha * u[k]) + beta * w[k]
        out_ref[0, :, here] = alpha * right[k] + alpha1 * direction
        out_ref[1, :, here] = res[k] - alpha1 * image

    hops = 2 * (nzh - 1)
    sent(rowbuf.at[0, : 2 * hops], 0)
    sent(rowbuf.at[0, : 4 * len(ls)], 1)
    sent(rowbuf.at[:, : 2 * (ny - 1) * nzl], 2)
    sent(rowbuf.at[:, : 2 * len(plane) * nzh], 3)
    sent(rowbuf.at[:, : 2 * len(plane) * nzh], 4)
    counts = [ncol - 1 if DIRECT[it] else (ny - 1) * nzl for it in range(2)]
    sent(rowbuf.at[0, : 2 * sum(counts)], 5)
    extra = sum(0 if DIRECT[it] else nzl - 1 for it in range(2))
    sent(rowbuf.at[0, : 2 * (hops + extra)], 6)
    sent(red_dst, 7)


def local(
    rparts,
    cparts,
    right_sides,
    noise_var,
    observed,
    tile_data,
    diag_tiles,
    tile_rows,
    tile_cols,
    tile_count,
):
    slots = tile_data.shape[2]
    nzh, nx, nc = rparts
    ny, nzl = cparts
    nrow, ncol = nzh * nx * nc, ny * nzl
    plane = nx * nc - 1
    vmem = pl.BlockSpec(memory_space=pltpu.VMEM)
    hbm = pl.BlockSpec(memory_space=pltpu.HBM)
    dma = pltpu.SemaphoreType.DMA
    chunk = (2, NRHS, TILE)
    shape = jax.ShapeDtypeStruct((2, *right_sides.shape), F32)
    out = pl.pallas_call(
        functools.partial(kernel, rparts, cparts),
        out_shape=shape,
        in_specs=[hbm] * 8,
        out_specs=vmem,
        scratch_shapes=[
            pltpu.VMEM(right_sides.shape, F32),
            pltpu.VMEM((1, 2 * TILE), F32),
            pltpu.VMEM((1, 2 * TILE), jnp.int32),
            pltpu.SMEM((slots,), jnp.int32),
            pltpu.SMEM((slots,), jnp.int32),
            pltpu.SMEM((1, 1), jnp.int32),
            pltpu.VMEM((slots, TILE, TILE), BF16),
            pltpu.VMEM((2, TILE, TILE), BF16),
            pltpu.VMEM((2, TILE, TILE), BF16),
            pltpu.VMEM((2 * nrow * NRHS, slots * NRHS), BF16),
            pltpu.VMEM((2 * ncol * NRHS, slots * NRHS), BF16),
            pltpu.VMEM((2, 2 * nrow, NRHS, TILE), F32),
            pltpu.VMEM((2, 2 * ncol, NRHS, TILE), F32),
            pltpu.VMEM((2 * nrow, 2 * NRHS, TILE), BF16),
            pltpu.VMEM((2 * ncol, 2 * NRHS, TILE), BF16),
            pltpu.VMEM((slots * NRHS, 2 * TILE), BF16),
            pltpu.VMEM((2, nzh, 2 * nx * nc, NRHS, TILE), F32),
            pltpu.VMEM((2, 2 * ncol, NRHS, TILE), F32),
            pltpu.VMEM((2, nzh, plane, *chunk), F32),
            pltpu.VMEM((2, nzh, *chunk), F32),
            pltpu.VMEM((2, nzh - 1, *chunk), F32),
            pltpu.VMEM((2, ncol - 1, *chunk), F32),
            pltpu.VMEM((2, nzl - 1, *chunk), F32),
            pltpu.VMEM((2, nzl - 1, *chunk), F32),
            pltpu.VMEM((3, 2, 1, TILE), F32),
            pltpu.VMEM((3, (plane + 1) * ny - 1 + nzh * nzl - 1, 1, TILE), F32),
            dma((8,)),
            dma((8,)),
            dma((2, 3)),
            dma((2, 2)),
            dma((2, nzl - 1)),
            dma((2,)),
            dma((2, nzh)),
            dma((2,)),
            dma((2, 3)),
            dma((2,)),
            dma((3, 2)),
        ],
        compiler_params=pltpu.CompilerParams(
            collective_id=0,
            has_side_effects=True,
            vmem_limit_bytes=67043328,
        ),
        name="solve",
    )(
        right_sides,
        noise_var.reshape(1, -1),
        observed.reshape(1, -1),
        diag_tiles,
        tile_data.reshape(slots, TILE, TILE),
        tile_rows.reshape(slots),
        tile_cols.reshape(slots),
        tile_count,
    )
    return out[0], out[1]


def solution(mesh):
    return jax.shard_map(
        functools.partial(local, ROW_PARTS, COL_PARTS),
        mesh=mesh,
        in_specs=(
            P(None, ("row", "col")),
            P(("row", "col")),
            P(("row", "col")),
            P("row", "col", None, None, None),
            P(("row", "col"), None, None),
            P("row", "col", None),
            P("row", "col", None),
            P("row", "col"),
        ),
        out_specs=(P(None, ("row", "col")), P(None, ("row", "col"))),
        check_vma=False,
    )
```
